1024 devices in a mesh: grp: 8 (over y, core), seq: 32 (over z), rep: 4 (over x).
Axes of the slice: x: 4, y: 4, z: 32, core: 2. Of those that a mesh axis runs over, the one named last changes fastest.
Arguments:
- tokens: bfloat16 [131072, 2048], P(('rep', 'grp', 'seq')), parts along dimension 0, may hold values from -6 to 6
- token_cot: bfloat16 [131072, 2048], P(('rep', 'grp', 'seq')), parts along dimension 0, may hold values from -1.5 to 1.5
- router_logits: float32 [131072, 256], P(('rep', 'grp', 'seq')), parts along dimension 0, may hold values from -6 to 6
- token_lists: int32 [1024, 128], P('rep'), parts along dimension 0, may hold values from 0 to 32767, as said below
- w_gate: bfloat16 [256, 2048, 384], P(('grp', 'seq')), may hold values from -0.125 to 0.125
- w_up: bfloat16 [256, 2048, 384], P(('grp', 'seq')), may hold values from -0.125 to 0.125
- w_down: bfloat16 [256, 384, 2048], P(('grp', 'seq')), may hold values from -0.3125 to 0.3125
Outputs:
- token_grad: bfloat16 [131072, 2048], P(('rep', 'grp', 'seq')), parts along dimension 0
- logit_grad: float32 [131072, 256], P(('rep', 'grp', 'seq')), parts along dimension 0
The draws below stay inside these ranges and needn't reach their ends.
There are 4 independent parts, one for each index of `rep`. The reference program is written for one: setup_inputs(seed, part) draws one part's arguments, and reference() takes and returns one part's arrays. A program takes and returns all parts, laid end to end along the dimension named above; an argument that names none is the same for every part. Nothing has to cross between parts.
Inputs may be any that keep to these rules, and one draw needn't show every extreme that they name: `token_lists`: row e lists 128 distinct tokens, no two of them from the same device's block of 128 consecutive tokens.
All inputs are finite; a program needn't handle non-finite values.
Results may differ from the reference program's by a relative error of at most 0.007.
Values may be sent and summed in bfloat16 or wider, within the bound.
A program may use at most 32 MiB of HBM per device.

```python
import jax
import jax.numpy as jnp
from jax import lax

D = 2048
FF = 384
TOK_DEV = 128
SHARDS = 256
EXPERTS = 256
CAP = 128
TOKENS = 32768


def draw_token_lists(key, part):
    key_rank, key_jitter, key_local = jax.random.split(key, 3)
    ranking = jax.random.permutation(key_rank, SHARDS)
    is_hot = (ranking < SHARDS // 8).astype(jnp.int32)
    jitter_vals = jax.random.randint(key_jitter, (EXPERTS, SHARDS), 0, 1024)
    scores = is_hot[None, :] * (1 << 22) + jitter_vals * SHARDS + jnp.arange(SHARDS, dtype=jnp.int32)[None, :]
    unused_vals, chosen = lax.top_k(scores, CAP)
    local_ids = jax.random.randint(key_local, (EXPERTS, CAP), 0, TOK_DEV)
    return (chosen.astype(jnp.int32) * TOK_DEV + local_ids).astype(jnp.int32)


def levels(own_key, extent, pieces, low, top_value):
    level, own = 1.0, jax.random.fold_in(own_key, 6)
    for dim, parts in pieces:
        heights = jnp.exp(jax.random.uniform(jax.random.fold_in(own, dim), (parts,), jnp.float32, low / len(pieces), top_value / len(pieces)))
        level = level * jnp.repeat(heights, extent[dim] // parts).reshape([-1 if axis == dim else 1 for axis in range(len(extent))])
    return level


def normal_values(key, shape, width, bound, pieces=(), kind=jnp.bfloat16):
    drawn = width * jax.random.normal(key, shape, jnp.float32)
    if pieces:
        drawn = drawn * levels(key, shape, pieces, -0.22, 0.18)
    return jnp.clip(drawn, -bound, bound).astype(kind)


def setup_inputs(seed: int = 0, part: int = 0) -> dict:
    key_list = jax.random.split(jax.random.key(seed), 8)
    part_keys = jax.random.split(jax.random.fold_in(key_list[7], part), 8)
    return {
        "tokens": normal_values(part_keys[0], (TOKENS, D), 1.0, 6.0, ((0, 256),)),
        "token_cot": normal_values(part_keys[1], (TOKENS, D), 0.25, 1.5, ((0, 256),)),
        "router_logits": normal_values(part_keys[2], (TOKENS, EXPERTS), 1.5, 6.0, ((0, 256),), jnp.float32),
        "token_lists": draw_token_lists(jax.random.fold_in(jax.random.fold_in(key_list[7], part), 71), part),
        "w_gate": normal_values(key_list[4], (EXPERTS, D, FF), D ** -0.5, 0.125, ((0, 256),)),
        "w_up": normal_values(key_list[5], (EXPERTS, D, FF), D ** -0.5, 0.125, ((0, 256),)),
        "w_down": normal_values(key_list[6], (EXPERTS, FF, D), FF ** -0.5, 0.3125, ((0, 256),)),
    }


def expert_back(in_rows, cot_rows, gate_mat, up_mat, down_mat):
    gate_pre = jnp.dot(in_rows, gate_mat, preferred_element_type=jnp.float32)
    up_pre = jnp.dot(in_rows, up_mat, preferred_element_type=jnp.float32)
    sig_gate = jax.nn.sigmoid(gate_pre)
    activated = gate_pre * sig_gate
    hidden = (activated * up_pre).astype(jnp.bfloat16)
    expert_out = jnp.dot(hidden, down_mat, preferred_element_type=jnp.float32)
    gate_grads = jnp.sum(cot_rows.astype(jnp.float32) * expert_out, axis=-1).astype(jnp.bfloat16)
    d_hidden = lax.dot_general(cot_rows, down_mat, (((1,), (1,)), ((), ())), preferred_element_type=jnp.float32)
    d_gate = (d_hidden * up_pre * sig_gate * (1.0 + gate_pre * (1.0 - sig_gate))).astype(jnp.bfloat16)
    d_up = (d_hidden * activated).astype(jnp.bfloat16)
    row_grads = lax.dot_general(d_gate, gate_mat, (((1,), (1,)), ((), ())), preferred_element_type=jnp.float32)
    row_grads = row_grads + lax.dot_general(d_up, up_mat, (((1,), (1,)), ((), ())), preferred_element_type=jnp.float32)
    return row_grads.astype(jnp.bfloat16), gate_grads


def reference(tokens, token_cot, router_logits, token_lists, w_gate, w_up, w_down):
    gate_vals = jax.nn.sigmoid(router_logits)

    def per_expert(expert):
        row_ids = token_lists[expert]
        row_grads, gate_grads = expert_back(tokens[row_ids], token_cot[row_ids], w_gate[expert], w_up[expert], w_down[expert])
        gate_sel = gate_vals[row_ids, expert]
        return row_grads, gate_grads, gate_sel

    row_grads, gate_grads, gate_sel = lax.map(per_expert, jnp.arange(EXPERTS, dtype=jnp.int32))
    flat_ids = token_lists.reshape(-1)
    weighted = (gate_sel[:, :, None] * row_grads.astype(jnp.float32)).reshape(-1, D)
    token_grad = jnp.zeros((TOKENS, D), jnp.float32).at[flat_ids].add(weighted)
    logit_part = gate_sel * (1.0 - gate_sel) * gate_grads.astype(jnp.float32)
    expert_ids = jnp.broadcast_to(jnp.arange(EXPERTS, dtype=jnp.int32)[:, None], token_lists.shape)
    logit_grad = jnp.zeros((TOKENS, EXPERTS), jnp.float32).at[flat_ids, expert_ids.reshape(-1)].add(logit_part.reshape(-1))
    return token_grad.astype(jnp.bfloat16), logit_grad
```

```python
import functools

import jax
import jax.numpy as jnp
from jax import lax
from jax.experimental import pallas as pl
from jax.experimental.pallas import tpu as pltpu
from jax.sharding import PartitionSpec as P

MESH = pl.DeviceIdType.MESH
BF16 = jnp.bfloat16
F32 = jnp.float32


def up16(n):
    return -(-n // 16) * 16


def one_hot_rows(pos_row, rows):
    row_ids = lax.broadcasted_iota(jnp.int32, (rows, pos_row.shape[1]), 0)
    return jnp.where(row_ids == pos_row, 1.0, 0.0).astype(BF16)


def ring_kernel(
    dims, caps,
    x_ref, g_ref, hot_ref, pos_ref, wg_hbm, wu_hbm, wd_hbm,
    fin_ref,
    wg_ref, wu_ref, wd_ref, send_buf, own, pack, final, gate_scr, up_scr, dxg, *rest,
):
    n_grp, n_seq, width, tail = dims
    half = n_seq // 2
    spc = half // 2
    wide = width + tail
    back = rest[:half]
    acc, back_send, w_sem, s1_send, s1_recv, d_send, d_recv, r_send, r_recv, s2_send, s2_recv, loc_sem = rest[half:]
    packs = (pack,) if not isinstance(pack, (tuple, list)) else pack
    lanes = n_grp * half
    grp = lax.axis_index("grp")
    col = lax.axis_index("seq")
    cap_last = caps[half - 1]

    def neighbour(direction):
        return lax.rem(col + 1 + direction * (n_seq - 2), n_seq)

    def peer(step):
        return lax.rem(grp + step, n_grp)

    weights = [
        pltpu.make_async_copy(wg_hbm, wg_ref, w_sem.at[0]),
        pltpu.make_async_copy(wu_hbm, wu_ref, w_sem.at[1]),
        pltpu.make_async_copy(wd_hbm, wd_ref, w_sem.at[2]),
    ]
    for copy in weights:
        copy.start()

    barrier = pltpu.get_barrier_semaphore()
    for step in range(1, n_grp):
        pl.semaphore_signal(barrier, inc=1, device_id={"grp": peer(step)}, device_id_type=MESH)
    for direction in range(2):
        pl.semaphore_signal(barrier, inc=1, device_id={"seq": neighbour(direction)}, device_id_type=MESH)

    col_tile = min(width, 512)
    n_tiles = width // col_tile

    def pick(source, arr, chunk):
        hot = hot_ref[pl.ds(chunk * lanes, lanes), :]

        def tile(i, carry):
            cols = pl.ds(pl.multiple_of(i * col_tile, col_tile), col_tile)
            rows = jnp.dot(hot, source[:, cols], preferred_element_type=F32).astype(BF16)
            send_buf[arr, chunk, :, :, cols] = rows.reshape(n_grp, half, col_tile)
            return carry

        lax.fori_loop(0, n_tiles, tile, 0)

    def stage_copy(arr, chunk, step):
        return pltpu.make_async_remote_copy(
            src_ref=send_buf.at[arr, chunk, peer(step)],
            dst_ref=own.at[arr, chunk, grp],
            send_sem=s1_send.at[arr, chunk, step],
            recv_sem=s1_recv.at[arr, chunk, step],
            device_id={"grp": peer(step)},
            device_id_type=MESH,
        )

    def stage_arrival(arr, chunk, step):
        return pltpu.make_async_remote_copy(
            src_ref=send_buf.at[arr, chunk, peer(step)],
            dst_ref=own.at[arr, chunk, lax.rem(grp + n_grp - step, n_grp)],
            send_sem=s1_send.at[arr, chunk, step],
            recv_sem=s1_recv.at[arr, chunk, step],
            device_id={"grp": peer(step)},
            device_id_type=MESH,
        )

    def stage_local(arr, chunk):
        return pltpu.make_async_copy(
            send_buf.at[arr, chunk, grp], own.at[arr, chunk, grp], loc_sem.at[arr, chunk]
        )

    pick(x_ref, 0, 0)
    pick(g_ref, 1, 0)
    pl.semaphore_wait(barrier, n_grp + 1)
    for chunk in range(2):
        for arr in range(2):
            if chunk == 1:
                pick((x_ref, g_ref)[arr], arr, chunk)
            stage_local(arr, chunk).start()
            for step in range(1, n_grp):
                stage_copy(arr, chunk, step).start()

    def own_rows(arr, chunk, cols):
        return own[arr, chunk, :, :, cols].reshape(lanes, col_tile)

    def packet(step):
        return packs[step]

    def send_packet(step, arr, direction):
        src = packet(step).at[arr, direction]
        if step + 1 < half:
            dst = packet(step + 1).at[arr, direction, pl.ds(0, caps[step])]
        else:
            dst = final.at[arr, pl.ds(direction * cap_last, cap_last)]
        return pltpu.make_async_remote_copy(
            src_ref=src,
            dst_ref=dst,
            send_sem=d_send.at[arr, direction, step],
            recv_sem=d_recv.at[arr, direction, step],
            device_id={"seq": neighbour(direction)},
            device_id_type=MESH,
        )

    for step in range(half):
        chunk = step // spc
        cap = caps[step]
        prev_cap = caps[step - 1] if step else 0
        for arr in range(2):
            if step % spc == 0:
                stage_local(arr, chunk).wait()
                for s in range(1, n_grp):
                    stage_arrival(arr, chunk, s).wait_recv()

            def hop(direction, carry, step=step, arr=arr, chunk=chunk, cap=cap, prev_cap=prev_cap):
                if step:
                    send_packet(step - 1, arr, direction).wait_recv()
                hot = one_hot_rows(pos_ref[pl.ds(2 * step + direction, 1), :], cap)

                def tile(i, inner):
                    cols = pl.ds(pl.multiple_of(i * col_tile, col_tile), col_tile)
                    rows = jnp.dot(hot, own_rows(arr, chunk, cols), preferred_element_type=F32)
                    target = packet(step)
                    if prev_cap:
                        held = target[arr, direction, pl.ds(0, prev_cap), cols].astype(F32)
                        target[arr, direction, pl.ds(0, prev_cap), cols] = (held + rows[:prev_cap]).astype(BF16)
                    if cap > prev_cap:
                        target[arr, direction, pl.ds(prev_cap, cap - prev_cap), cols] = rows[prev_cap:].astype(BF16)
                    return inner

                lax.fori_loop(0, n_tiles, tile, 0)
                send_packet(step, arr, direction).start()
                return carry

            lax.fori_loop(0, 2, hop, 0)

    for arr in range(2):
        hot = one_hot_rows(pos_ref[pl.ds(2 * half, 1), :], 16)

        def tile(i, inner, arr=arr, hot=hot):
            cols = pl.ds(pl.multiple_of(i * col_tile, col_tile), col_tile)
            rows = jnp.dot(hot, own_rows(arr, 0, cols), preferred_element_type=F32)
            final[arr, pl.ds(2 * cap_last, 16), cols] = rows.astype(BF16)
            return inner

        lax.fori_loop(0, n_tiles, tile, 0)

    for copy in weights:
        copy.wait()
    for direction in range(2):
        send_packet(half - 1, 0, direction).wait_recv()
    gate_scr[...] = jnp.dot(final[0], wg_ref[...], preferred_element_type=F32)
    up_scr[...] = jnp.dot(final[0], wu_ref[...], preferred_element_type=F32)
    for direction in range(2):
        send_packet(half - 1, 1, direction).wait_recv()
    nt = (((1,), (1,)), ((), ()))
    d_hidden = lax.dot_general(final[1], wd_ref[...], nt, preferred_element_type=F32)
    gate_pre = gate_scr[...]
    up_pre = up_scr[...]
    sig = jax.nn.sigmoid(gate_pre)
    activated = gate_pre * sig
    hidden = (activated * up_pre).astype(BF16).astype(F32)
    gate_grad = jnp.sum(hidden * d_hidden, axis=1, keepdims=True)
    d_gate = (d_hidden * up_pre * sig * (1.0 + gate_pre * (1.0 - sig))).astype(BF16)
    d_up = (d_hidden * activated).astype(BF16)
    gate_scr[...] = d_gate.astype(F32)
    up_scr[...] = d_up.astype(F32)
    dxg[:, width:] = jnp.broadcast_to(gate_grad, (gate_grad.shape[0], tail)).astype(BF16)

    def dx_tile(i, carry):
        cols = pl.ds(pl.multiple_of(i * col_tile, col_tile), col_tile)
        rows = lax.dot_general(gate_scr[...].astype(BF16), wg_ref[cols, :], nt, preferred_element_type=F32)
        rows = rows + lax.dot_general(up_scr[...].astype(BF16), wu_ref[cols, :], nt, preferred_element_type=F32)
        dxg[:, cols] = rows.astype(BF16)
        return carry

    lax.fori_loop(0, n_tiles, dx_tile, 0)

    def send_back(step, direction):
        cap = caps[half - 1 - step]
        if step == 0:
            src = dxg.at[pl.ds(direction * cap_last, cap_last)]
        else:
            src = back[step - 1].at[direction, pl.ds(0, cap)]
        return pltpu.make_async_remote_copy(
            src_ref=src,
            dst_ref=back[step].at[direction],
            send_sem=r_send.at[direction, step],
            recv_sem=r_recv.at[direction, step],
            device_id={"seq": neighbour(1 - direction)},
            device_id_type=MESH,
        )

    def home_copy(chunk, step, src_grp):
        return pltpu.make_async_remote_copy(
            src_ref=back_send.at[chunk, peer(step)],
            dst_ref=fin_ref.at[chunk, src_grp],
            send_sem=s2_send.at[chunk, step],
            recv_sem=s2_recv.at[chunk, step],
            device_id={"grp": peer(step)},
            device_id_type=MESH,
        )

    def home_local(chunk):
        return pltpu.make_async_copy(back_send.at[chunk, grp], fin_ref.at[chunk, grp], loc_sem.at[2, chunk])

    tn = (((0,), (0,)), ((), ()))

    def add_rows(chunk, hot, load):
        def tile(i, inner):
            cols = pl.ds(pl.multiple_of(i * col_tile, col_tile), col_tile)
            acc[:, cols] += lax.dot_general(hot, load(cols), tn, preferred_element_type=F32)
            return inner

        lax.fori_loop(0, n_tiles, tile, 0)
        last = pl.ds(width, tail)
        acc[:, last] += lax.dot_general(hot, load(last), tn, preferred_element_type=F32)

    for direction in range(2):
        send_back(0, direction).start()
    for step in range(half):
        chunk = 1 if step < spc else 0
        cap = caps[half - 1 - step]
        if step == 0:
            acc[...] = jnp.zeros_like(acc)
        if step == spc:
            acc[...] = jnp.zeros_like(acc)
            hot = one_hot_rows(pos_ref[pl.ds(2 * half, 1), :], 16)
            add_rows(0, hot, lambda cols: dxg[pl.ds(2 * cap_last, 16), cols])
        for direction in range(2):
            send_back(step, direction).wait_recv()
            if step + 1 < half:
                send_back(step + 1, direction).start()

        def drop(direction, carry, step=step, cap=cap, chunk=chunk):
            row = 2 * (half - 1 - step) + direction
            hot = one_hot_rows(pos_ref[pl.ds(row, 1), :], cap)
            add_rows(chunk, hot, lambda cols: back[step][direction, :, cols])
            return carry

        lax.fori_loop(0, 2, drop, 0)
        if step in (spc - 1, half - 1):
            back_send[chunk] = acc[...].astype(BF16).reshape(n_grp, half, wide)
            home_local(chunk).start()
            for s in range(1, n_grp):
                home_copy(chunk, s, grp).start()

    for chunk in range(2):
        home_local(chunk).wait()
        for s in range(1, n_grp):
            home_copy(chunk, s, lax.rem(grp + n_grp - s, n_grp)).wait_recv()
            home_copy(chunk, s, grp).wait_send()
        for arr in range(2):
            for s in range(1, n_grp):
                stage_copy(arr, chunk, s).wait_send()
    for step in range(half):
        for direction in range(2):
            for arr in range(2):
                send_packet(step, arr, direction).wait_send()
            send_back(step, direction).wait_send()


def entry(dims, caps, n_packs, *refs):
    ins, out, mid, rest = refs[:7], refs[7], refs[8:13], refs[13:]
    packs = rest[:n_packs]
    ring_kernel(dims, caps, *ins, out, *mid, packs, *rest[n_packs:])


def exchange(dims, caps, collective_id, tokens, token_cot, hot, pos, w_gate, w_up, w_down):
    n_grp, n_seq, width, tail = dims
    half = n_seq // 2
    ff = w_gate.shape[1]
    wide = width + tail
    rows = 2 * caps[-1] + 16
    lanes = n_grp * half
    dma = pltpu.SemaphoreType.DMA
    vmem = pl.BlockSpec(memory_space=pltpu.VMEM)
    hbm = pl.BlockSpec(memory_space=pl.ANY)
    scratch = [
        pltpu.VMEM(w_gate.shape, BF16),
        pltpu.VMEM(w_up.shape, BF16),
        pltpu.VMEM(w_down.shape, BF16),
        pltpu.VMEM((2, 2, n_grp, half, width), BF16),
        pltpu.VMEM((2, 2, n_grp, half, width), BF16),
        *[pltpu.VMEM((2, 2, cap, width), BF16) for cap in caps],
        pltpu.VMEM((2, rows, width), BF16),
        pltpu.VMEM((rows, ff), F32),
        pltpu.VMEM((rows, ff), F32),
        pltpu.VMEM((rows, wide), BF16),
        *[pltpu.VMEM((2, cap, wide), BF16) for cap in reversed(caps)],
        pltpu.VMEM((lanes, wide), F32),
        pltpu.VMEM((2, n_grp, half, wide), BF16),
        dma((3,)),
        dma((2, 2, n_grp)),
        dma((2, 2, n_grp)),
        dma((2, 2, half)),
        dma((2, 2, half)),
        dma((2, half)),
        dma((2, half)),
        dma((2, n_grp)),
        dma((2, n_grp)),
        dma((3, 2)),
    ]
    return pl.pallas_call(
        functools.partial(entry, dims, caps, half),
        out_shape=jax.ShapeDtypeStruct((2, n_grp, half, wide), BF16),
        in_specs=[vmem, vmem, vmem, vmem, hbm, hbm, hbm],
        out_specs=vmem,
        scratch_shapes=scratch,
        compiler_params=pltpu.CompilerParams(
            collective_id=collective_id, has_side_effects=True, vmem_limit_bytes=60 * 1024 * 1024
        ),
        name=f"ring_exchange_{collective_id}",
    )(tokens, token_cot, hot, pos, w_gate, w_up, w_down)


def to_slots(values, half):
    spc = half // 2
    first = jnp.concatenate(
        [jnp.flip(values[:, spc + 1 : half + 1], 1), values[:, :1], values[:, half + 1 : half + spc]], axis=1
    )
    second = jnp.concatenate([jnp.flip(values[:, 1 : spc + 1], 1), values[:, half + spc :]], axis=1)
    return jnp.stack([first, second])


def from_slots(slots, half):
    spc = half // 2
    first, second = slots[0], slots[1]
    return jnp.concatenate(
        [
            first[:, spc : spc + 1],
            jnp.flip(second[:, :spc], 1),
            jnp.flip(first[:, :spc], 1),
            first[:, spc + 1 :],
            second[:, spc:],
        ],
        axis=1,
    )


def roll_columns(values, start):
    doubled = jnp.concatenate([values, values], axis=1)
    return lax.dynamic_slice_in_dim(doubled, start, values.shape[1], axis=1)


def ring_positions(lists, tok_rows, n_grp, n_seq, col):
    half = n_seq // 2
    spc = half // 2
    owner = lists // tok_rows
    src = owner // n_seq
    off = lax.rem(owner % n_seq - col + n_seq, n_seq)
    here = off == 0
    dest = jnp.arange(n_seq, dtype=jnp.int32)[:, None]
    low = src < n_grp // 2
    d_up = lax.rem(dest - off + n_seq, n_seq)
    d_down = lax.rem(off - dest + n_seq, n_seq)
    in_up = (d_up < half) | ((d_up == half) & low)
    in_down = (d_down < half) | ((d_down == half) & ~low)
    groups = jnp.arange(n_grp, dtype=jnp.int32)

    def positions(inside, distance, own_distance):
        ahead = (inside & (distance > own_distance))[:, :, None]
        mine = (inside & here)[:, :, None]
        before = mine & (src[:, :, None] < groups)
        place = jnp.sum((ahead | before).astype(jnp.int32), axis=1)
        present = jnp.any(mine & (src[:, :, None] == groups), axis=1)
        return jnp.where(present, place, -1)

    up = jnp.flip(positions(in_up, d_up, dest)[1 : half + 1], 0)
    down = positions(in_down, d_down, n_seq - dest)[half:]
    by_step = jnp.stack([up, down], axis=1).reshape(n_seq, n_grp)
    same = jnp.any(here[0][:, None] & (src[0][:, None] == groups), axis=0)
    by_step = jnp.concatenate([by_step, jnp.where(same, groups, -1)[None, :]], axis=0)
    slot = [(k % spc) + spc * direction for k in range(half) for direction in range(2)]
    slot[1] = 0
    slot = jnp.array(slot + [spc], jnp.int32)
    at_slot = slot[:, None, None] == jnp.arange(half, dtype=jnp.int32)
    table = jnp.where(at_slot, by_step[:, :, None], -1).reshape(n_seq + 1, n_grp * half)
    return jnp.pad(table, ((0, 7), (0, 0)), constant_values=-1)


def body(tokens, token_cot, router_logits, token_lists, w_gate, w_up, w_down):
    n_grp = lax.axis_size("grp")
    n_seq = lax.axis_size("seq")
    half = n_seq // 2
    grp = lax.axis_index("grp")
    col = lax.axis_index("seq")
    tok_rows, width = tokens.shape
    n_experts, cap = token_lists.shape
    dims = (n_grp, n_seq, width, 128)

    token_ids = jnp.arange(tok_rows, dtype=jnp.int32)
    local = token_lists - (grp * n_seq + col) * tok_rows
    mine = (local >= 0) & (local < tok_rows)
    picked = jnp.max(jnp.where(mine, local, -1), axis=1)
    slots = to_slots(roll_columns(picked.reshape(n_grp, n_seq), col), half)
    hot = (slots.reshape(n_experts)[:, None] == token_ids).astype(BF16)

    ring_lists = lax.dynamic_slice_in_dim(token_lists, grp * n_seq, n_seq, axis=0)
    ring_lists = jnp.concatenate([ring_lists, ring_lists], axis=0)
    ring_lists = lax.dynamic_slice_in_dim(ring_lists, col, n_seq, axis=0)
    pos = ring_positions(ring_lists, tok_rows, n_grp, n_seq, col)

    full = tuple(up16(n_grp * k - n_grp // 2) for k in range(1, half + 1))
    fin = exchange(dims, full, 0, tokens, token_cot, hot, pos, w_gate[0], w_up[0], w_down[0])
    fin = fin.reshape(n_experts, width + dims[3])

    gate_vals = jax.nn.sigmoid(router_logits)
    select = picked[None, :] == token_ids[:, None]
    own_gates = jnp.sum(jnp.where(select, gate_vals, 0.0), axis=0)
    gate_slots = to_slots(roll_columns(own_gates.reshape(n_grp, n_seq), col), half).reshape(n_experts)
    weight = jnp.where(slots.reshape(n_experts)[:, None] == token_ids, gate_slots[:, None], 0.0)
    token_grad = lax.dot_general(
        weight,
        fin[:, :width].astype(F32),
        (((0,), (0,)), ((), ())),
        precision=lax.Precision.HIGHEST,
        preferred_element_type=F32,
    )
    back_gates = from_slots(fin[:, width].reshape(2, n_grp, half), half)
    back_gates = roll_columns(back_gates, lax.rem(n_seq - col, n_seq)).reshape(n_experts).astype(F32)
    logit_grad = jnp.where(select, gate_vals * (1.0 - gate_vals) * back_gates[None, :], 0.0)
    return (token_grad.astype(BF16), logit_grad)


def solution(mesh):
    in_specs = (
        P(("rep", "grp", "seq"), None),
        P(("rep", "grp", "seq"), None),
        P(("rep", "grp", "seq"), None),
        P("rep", None),
        P(("grp", "seq"), None, None),
        P(("grp", "seq"), None, None),
        P(("grp", "seq"), None, None),
    )
    out_specs = (P(("rep", "grp", "seq"), None), P(("rep", "grp", "seq"), None))
    return jax.shard_map(body, mesh=mesh, in_specs=in_specs, out_specs=out_specs, check_vma=False)
```

```python
import functools
import math

import jax
import jax.numpy as jnp
from jax import lax
from jax.experimental import pallas as pl
from jax.experimental.pallas import tpu as pltpu
from jax.sharding import PartitionSpec as P

MESH = pl.DeviceIdType.MESH
BF16 = jnp.bfloat16
F32 = jnp.float32


def up16(n):
    return -(-n // 16) * 16


def usual_caps(n_grp, n_seq):
    total = n_grp * n_seq
    caps = []
    for k in range(1, n_seq // 2 + 1):
        slots = n_grp * k - n_grp // 2
        spread = math.sqrt(slots * (total - slots) / (4 * total))
        caps.append(-(-math.floor(min(slots, slots / 2 + 4.75 * spread)) // 8) * 8)
    return tuple(max(cap, caps[0]) for cap in caps)


def one_hot_rows(pos_row, rows):
    row_ids = lax.broadcasted_iota(jnp.int32, (rows, pos_row.shape[1]), 0)
    return jnp.where(row_ids == pos_row, 1.0, 0.0).astype(BF16)


def ring_kernel(dims, caps, ins, fin_ref, scratch):
    n_grp, n_seq, width, tail = dims
    half = n_seq // 2
    spc = half // 2
    wide = width + tail
    lanes = n_grp * half
    x_ref, g_ref, hot_ref, pos_ref, src_pos_ref, wg_hbm, wu_hbm, wd_hbm = ins
    packs, backs = scratch["packs"], (scratch["backs_a"], scratch["backs_b"])
    wg_ref, wu_ref, wd_ref = scratch["wg"], scratch["wu"], scratch["wd"]
    send_buf, own, fresh, final = scratch["send_buf"], scratch["own"], scratch["fresh"], scratch["final"]
    gate_scr, up_scr, dx = scratch["gate"], scratch["up"], (scratch["dx_a"], scratch["dx_b"])
    dropped, back_send = scratch["dropped"], scratch["back_send"]
    parts = ((0, width // 2), (width // 2, wide - width // 2))
    grp = lax.axis_index("grp")
    col = lax.axis_index("seq")
    cap_last = caps[half - 1]
    col_tile = min(width // 2, 512)
    n_tiles = width // col_tile

    def tile_cols(i):
        return pl.ds(pl.multiple_of(i * col_tile, col_tile), col_tile)

    def neighbour(direction):
        return lax.rem(col + 1 + direction * (n_seq - 2), n_seq)

    def peer(step):
        return lax.rem(grp + step, n_grp)

    weights = [
        pltpu.make_async_copy(wg_hbm, wg_ref, scratch["w_sem"].at[0]),
        pltpu.make_async_copy(wu_hbm, wu_ref, scratch["w_sem"].at[1]),
        pltpu.make_async_copy(wd_hbm, wd_ref, scratch["w_sem"].at[2]),
    ]

    barrier = pltpu.get_barrier_semaphore()
    for step in range(1, n_grp):
        pl.semaphore_signal(barrier, inc=1, device_id={"grp": peer(step)}, device_id_type=MESH)
    for direction in range(2):
        pl.semaphore_signal(barrier, inc=1, device_id={"seq": neighbour(direction)}, device_id_type=MESH)

    def pick(source, arr, chunk):
        hot = hot_ref[pl.ds(chunk * lanes, lanes), :]

        def tile(i, carry):
            cols = tile_cols(i)
            rows = jnp.dot(hot, source[:, cols], preferred_element_type=F32).astype(BF16)
            send_buf[arr, chunk, :, :, cols] = rows.reshape(n_grp, half, col_tile)
            return carry

        lax.fori_loop(0, n_tiles, tile, 0)

    def stage_copy(arr, chunk, step, src_grp):
        return pltpu.make_async_remote_copy(
            src_ref=send_buf.at[arr, chunk, peer(step)],
            dst_ref=own.at[arr, chunk, src_grp],
            send_sem=scratch["s1_send"].at[arr, chunk, step],
            recv_sem=scratch["s1_recv"].at[arr, chunk, step],
            device_id={"grp": peer(step)},
            device_id_type=MESH,
        )

    def stage_local(arr, chunk):
        return pltpu.make_async_copy(
            send_buf.at[arr, chunk, grp], own.at[arr, chunk, grp], scratch["loc_sem"].at[arr, chunk]
        )

    def stage_wait(arr, chunk):
        stage_local(arr, chunk).wait()
        for step in range(1, n_grp):
            stage_copy(arr, chunk, step, lax.rem(grp + n_grp - step, n_grp)).wait_recv()

    pick(x_ref, 0, 0)
    pl.semaphore_wait(barrier, n_grp + 1)
    for chunk, arr in ((0, 0), (0, 1), (1, 0), (1, 1)):
        if chunk or arr:
            pick((x_ref, g_ref)[arr], arr, chunk)
        stage_local(arr, chunk).start()
        for step in range(1, n_grp):
            stage_copy(arr, chunk, step, grp).start()
    for copy in weights:
        copy.start()

    def send_packet(step, arr, direction):
        if step + 1 < half:
            dst = packs[step + 1].at[arr, direction, pl.ds(0, caps[step])]
        else:
            dst = final.at[arr, pl.ds(direction * cap_last, cap_last)]
        return pltpu.make_async_remote_copy(
            src_ref=packs[step].at[arr, direction],
            dst_ref=dst,
            send_sem=scratch["d_send"].at[arr, direction, step],
            recv_sem=scratch["d_recv"].at[arr, direction, step],
            device_id={"seq": neighbour(direction)},
            device_id_type=MESH,
        )

    def make_fresh(step, arr):
        cap = caps[step]
        prev_cap = caps[step - 1] if step else 0

        def one(direction, carry):
            hot = one_hot_rows(pos_ref[pl.ds(2 * step + direction, 1), :], cap)

            def tile(i, inner):
                cols = tile_cols(i)
                mine = own[arr, step // spc, :, :, cols].reshape(lanes, col_tile)
                rows = jnp.dot(hot, mine, preferred_element_type=F32).astype(BF16)
                if prev_cap:
                    fresh[arr, direction, pl.ds(0, prev_cap), cols] = rows[:prev_cap]
                if cap > prev_cap:
                    packs[step][arr, direction, pl.ds(prev_cap, cap - prev_cap), cols] = rows[prev_cap:]
                return inner

            lax.fori_loop(0, n_tiles, tile, 0)
            return carry

        lax.fori_loop(0, 2, one, 0)

    for step in range(half):
        for arr in range(2):
            if step == 0:
                stage_wait(arr, 0)
                make_fresh(0, arr)

            def hop(direction, carry, step=step, arr=arr):
                if step:
                    prev = pl.ds(0, caps[step - 1])
                    send_packet(step - 1, arr, direction).wait_recv()
                    packs[step][arr, direction, prev, :] += fresh[arr, direction, prev, :]
                send_packet(step, arr, direction).start()
                return carry

            lax.fori_loop(0, 2, hop, 0)
            if step + 1 < half:
                if step + 1 == spc:
                    stage_wait(arr, 1)
                make_fresh(step + 1, arr)

    same_hot = one_hot_rows(pos_ref[pl.ds(2 * half, 1), :], 16)
    for arr in range(2):

        def same_tile(i, inner, arr=arr):
            cols = tile_cols(i)
            mine = own[arr, 0, :, :, cols].reshape(lanes, col_tile)
            rows = jnp.dot(same_hot, mine, preferred_element_type=F32)
            final[arr, pl.ds(2 * cap_last, 16), cols] = rows.astype(BF16)
            return inner

        lax.fori_loop(0, n_tiles, same_tile, 0)

    for copy in weights:
        copy.wait()
    for direction in range(2):
        send_packet(half - 1, 0, direction).wait_recv()
    gate_scr[...] = jnp.dot(final[0], wg_ref[...], preferred_element_type=F32)
    up_scr[...] = jnp.dot(final[0], wu_ref[...], preferred_element_type=F32)
    for direction in range(2):
        send_packet(half - 1, 1, direction).wait_recv()
    nt = (((1,), (1,)), ((), ()))
    d_hidden = lax.dot_general(final[1], wd_ref[...], nt, preferred_element_type=F32)
    gate_pre = gate_scr[...]
    up_pre = up_scr[...]
    sig = jax.nn.sigmoid(gate_pre)
    activated = gate_pre * sig
    hidden = (activated * up_pre).astype(BF16).astype(F32)
    gate_grad = jnp.sum(hidden * d_hidden, axis=1, keepdims=True)
    scratch["d_gate"][...] = (d_hidden * up_pre * sig * (1.0 + gate_pre * (1.0 - sig))).astype(BF16)
    scratch["d_up"][...] = (d_hidden * activated).astype(BF16)
    dx[1][:, width // 2 :] = jnp.broadcast_to(gate_grad, (gate_grad.shape[0], tail)).astype(BF16)

    def send_back(step, part, direction):
        cap = caps[half - 1 - step]
        if step == 0:
            src = dx[part].at[pl.ds(direction * cap_last, cap_last)]
        else:
            src = backs[part][step - 1].at[direction, pl.ds(0, cap)]
        return pltpu.make_async_remote_copy(
            src_ref=src,
            dst_ref=backs[part][step].at[direction],
            send_sem=scratch["r_send"].at[part, direction, step],
            recv_sem=scratch["r_recv"].at[part, direction, step],
            device_id={"seq": neighbour(1 - direction)},
            device_id_type=MESH,
        )

    for part in range(2):

        def dx_tile(i, carry, part=part):
            w_rows = tile_cols(i + part * (n_tiles // 2))
            rows = lax.dot_general(scratch["d_gate"][...], wg_ref[w_rows, :], nt, preferred_element_type=F32)
            rows = rows + lax.dot_general(scratch["d_up"][...], wu_ref[w_rows, :], nt, preferred_element_type=F32)
            dx[part][:, tile_cols(i)] = rows.astype(BF16)
            return carry

        lax.fori_loop(0, n_tiles // 2, dx_tile, 0)
        for direction in range(2):
            send_back(0, part, direction).start()

    def home_copy(chunk, step, src_grp):
        return pltpu.make_async_remote_copy(
            src_ref=back_send.at[chunk, peer(step)],
            dst_ref=fin_ref.at[chunk, src_grp],
            send_sem=scratch["s2_send"].at[chunk, step],
            recv_sem=scratch["s2_recv"].at[chunk, step],
            device_id={"grp": peer(step)},
            device_id_type=MESH,
        )

    def home_local(chunk):
        return pltpu.make_async_copy(back_send.at[chunk, grp], fin_ref.at[chunk, grp], scratch["loc_sem"].at[2, chunk])

    tn = (((0,), (0,)), ((), ()))

    def drop(row, cap, rows, slot, part, add=False):
        hot = one_hot_rows(src_pos_ref[pl.ds(row, 1), :n_grp], cap)
        first, size = parts[part]
        kept = lax.dot_general(hot, rows, tn, preferred_element_type=F32)
        at = pl.ds(slot * n_grp, n_grp)
        if add:
            kept = kept + dropped[at, pl.ds(first, size)]
        dropped[at, pl.ds(first, size)] = kept

    def regroup(chunk):
        shape = (lanes, lanes)
        to = lax.broadcasted_iota(jnp.int32, shape, 0)
        frm = lax.broadcasted_iota(jnp.int32, shape, 1)
        perm = jnp.where((to // half == frm % n_grp) & (to % half == frm // n_grp), 1.0, 0.0).astype(BF16)

        def put(cols, size):
            rows = jnp.dot(perm, dropped[:, cols].astype(BF16), preferred_element_type=F32).astype(BF16)
            back_send[chunk, :, :, cols] = rows.reshape(n_grp, half, size)

        def tile(i, carry):
            put(tile_cols(i), col_tile)
            return carry

        lax.fori_loop(0, n_tiles, tile, 0)
        put(pl.ds(width, tail), tail)

    for step in range(half):
        chunk = 1 if step < spc else 0
        k = half - 1 - step
        for part in range(2):
            for direction in range(2):
                send_back(step, part, direction).wait_recv()
                if step + 1 < half:
                    send_back(step + 1, part, direction).start()
            if step == spc:
                drop(2 * half, 16, dx[part][pl.ds(2 * cap_last, 16), :], spc, part)
            for direction in range(2):
                slot = k % spc + (spc if direction and k else 0)
                drop(2 * k + direction, caps[k], backs[part][step][direction], slot, part, bool(direction and k == 0))
        if step in (spc - 1, half - 1):
            regroup(chunk)
            home_local(chunk).start()
            for s in range(1, n_grp):
                home_copy(chunk, s, grp).start()

    for arr in range(2):
        for chunk in range(2):
            for s in range(1, n_grp):
                stage_copy(arr, chunk, s, grp).wait_send()
    for step in range(half):
        for direction in range(2):
            for arr in range(2):
                send_packet(step, arr, direction).wait_send()
                send_back(step, arr, direction).wait_send()
    for chunk in (1, 0):
        home_local(chunk).wait()
        for s in range(1, n_grp):
            home_copy(chunk, s, grp).wait_send()
            home_copy(chunk, s, lax.rem(grp + n_grp - s, n_grp)).wait_recv()


N_INS = 8


def exchange(dims, caps, collective_id, *operands):
    n_grp, n_seq, width, tail = dims
    half = n_seq // 2
    w_gate, w_up, w_down = operands[5:]
    ff = w_gate.shape[1]
    wide = width + tail
    rows = 2 * caps[-1] + 16
    lanes = n_grp * half
    dma = pltpu.SemaphoreType.DMA
    vmem = pl.BlockSpec(memory_space=pltpu.VMEM)
    hbm = pl.BlockSpec(memory_space=pl.ANY)
    scratch = {
        "wg": pltpu.VMEM(w_gate.shape, BF16),
        "wu": pltpu.VMEM(w_up.shape, BF16),
        "wd": pltpu.VMEM(w_down.shape, BF16),
        "send_buf": pltpu.VMEM((2, 2, n_grp, half, width), BF16),
        "own": pltpu.VMEM((2, 2, n_grp, half, width), BF16),
        "packs": [pltpu.VMEM((2, 2, cap, width), BF16) for cap in caps],
        "fresh": pltpu.VMEM((2, 2, caps[-2], width), BF16),
        "final": pltpu.VMEM((2, rows, width), BF16),
        "gate": pltpu.VMEM((rows, ff), F32),
        "up": pltpu.VMEM((rows, ff), F32),
        "d_gate": pltpu.VMEM((rows, ff), BF16),
        "d_up": pltpu.VMEM((rows, ff), BF16),
        "dx_a": pltpu.VMEM((rows, width // 2), BF16),
        "dx_b": pltpu.VMEM((rows, wide - width // 2), BF16),
        "backs_a": [pltpu.VMEM((2, cap, width // 2), BF16) for cap in reversed(caps)],
        "backs_b": [pltpu.VMEM((2, cap, wide - width // 2), BF16) for cap in reversed(caps)],
        "dropped": pltpu.VMEM((lanes, wide), F32),
        "back_send": pltpu.VMEM((2, n_grp, half, wide), BF16),
        "w_sem": dma((3,)),
        "s1_send": dma((2, 2, n_grp)),
        "s1_recv": dma((2, 2, n_grp)),
        "d_send": dma((2, 2, half)),
        "d_recv": dma((2, 2, half)),
        "r_send": dma((2, 2, half)),
        "r_recv": dma((2, 2, half)),
        "s2_send": dma((2, n_grp)),
        "s2_recv": dma((2, n_grp)),
        "loc_sem": dma((3, 2)),
    }
    leaves, tree = jax.tree.flatten(scratch, is_leaf=lambda leaf: not isinstance(leaf, (dict, list)))

    def kernel(*refs):
        named = jax.tree.unflatten(tree, refs[N_INS + 1 :])
        ring_kernel(dims, caps, refs[:N_INS], refs[N_INS], named)

    return pl.pallas_call(
        kernel,
        out_shape=jax.ShapeDtypeStruct((2, n_grp, half, wide), BF16),
        in_specs=[vmem] * 5 + [hbm] * 3,
        out_specs=vmem,
        scratch_shapes=leaves,
        compiler_params=pltpu.CompilerParams(
            collective_id=collective_id, has_side_effects=True, vmem_limit_bytes=60 * 1024 * 1024
        ),
        name=f"ring_exchange_{collective_id}",
    )(*operands)


def to_slots(values, half):
    spc = half // 2
    first = jnp.concatenate(
        [jnp.flip(values[:, spc + 1 : half + 1], 1), values[:, :1], values[:, half + 1 : half + spc]], axis=1
    )
    second = jnp.concatenate([jnp.flip(values[:, 1 : spc + 1], 1), values[:, half + spc :]], axis=1)
    return jnp.stack([first, second])


def from_slots(slots, half):
    spc = half // 2
    first, second = slots[0], slots[1]
    return jnp.concatenate(
        [
            first[:, spc : spc + 1],
            jnp.flip(second[:, :spc], 1),
            jnp.flip(first[:, :spc], 1),
            first[:, spc + 1 :],
            second[:, spc:],
        ],
        axis=1,
    )


def roll_columns(values, start):
    doubled = jnp.concatenate([values, values], axis=1)
    return lax.dynamic_slice_in_dim(doubled, start, values.shape[1], axis=1)


def ring_positions(lists, tok_rows, n_grp, n_seq, col):
    half = n_seq // 2
    spc = half // 2
    owner = lists // tok_rows
    src = owner // n_seq
    off = (owner - col) & (n_seq - 1)
    here = off == 0
    dest = jnp.arange(n_seq, dtype=jnp.int32)[:, None]
    low = src < n_grp // 2
    d_up = (dest - off) & (n_seq - 1)
    d_down = (off - dest) & (n_seq - 1)
    in_up = (d_up < half) | ((d_up == half) & low)
    in_down = (d_down < half) | ((d_down == half) & ~low)
    groups = jnp.arange(n_grp, dtype=jnp.int32)

    def positions(inside, distance, own_distance):
        ahead = (inside & (distance > own_distance))[:, :, None]
        mine = (inside & here)[:, :, None]
        before = mine & (src[:, :, None] < groups)
        place = jnp.sum((ahead | before).astype(jnp.int32), axis=1)
        present = jnp.any(mine & (src[:, :, None] == groups), axis=1)
        return jnp.where(present, place, -1)

    up = jnp.flip(positions(in_up, d_up, dest)[1 : half + 1], 0)
    down = positions(in_down, d_down, n_seq - dest)[half:]
    by_step = jnp.stack([up, down], axis=1).reshape(n_seq, n_grp)
    same = jnp.any(here[0][:, None] & (src[0][:, None] == groups), axis=0)
    by_step = jnp.concatenate([by_step, jnp.where(same, groups, -1)[None, :]], axis=0)
    slot = [(k % spc) + spc * direction for k in range(half) for direction in range(2)]
    slot[1] = 0
    slot = jnp.array(slot + [spc], jnp.int32)
    at_slot = slot[:, None, None] == jnp.arange(half, dtype=jnp.int32)
    table = jnp.where(at_slot, by_step[:, :, None], -1).reshape(n_seq + 1, n_grp * half)
    return table, by_step


def lists_fit(lists, caps, tok_rows, n_grp, n_seq):
    half = n_seq // 2
    owner = lists // tok_rows
    low = owner // n_seq < n_grp // 2
    column = owner % n_seq
    dest = jnp.arange(lists.shape[0], dtype=jnp.int32)[:, None] % n_seq
    gap = (dest - column) & (n_seq - 1)
    d_up = jnp.where((gap < half) | ((gap == half) & low), gap, 0)
    gap = (column - dest) & (n_seq - 1)
    d_down = jnp.where((gap < half) | ((gap == half) & ~low), gap, 0)
    least = half - jnp.arange(half, dtype=jnp.int32)
    limit = jnp.array(caps, jnp.int32)
    worst = 0
    for distance in (d_up, d_down):
        count = jnp.sum((distance[:, None, :] >= least[:, None]).astype(jnp.int32), axis=2)
        worst = jnp.maximum(worst, jnp.max(count - limit))
    return worst <= 0


def body(tokens, token_cot, router_logits, token_lists, w_gate, w_up, w_down):
    n_grp = lax.axis_size("grp")
    n_seq = lax.axis_size("seq")
    half = n_seq // 2
    grp = lax.axis_index("grp")
    col = lax.axis_index("seq")
    tok_rows, width = tokens.shape
    n_experts, cap = token_lists.shape
    dims = (n_grp, n_seq, width, 128)

    token_ids = jnp.arange(tok_rows, dtype=jnp.int32)
    local = token_lists - (grp * n_seq + col) * tok_rows
    mine = (local >= 0) & (local < tok_rows)
    picked = jnp.max(jnp.where(mine, local, -1), axis=1)
    slots = to_slots(roll_columns(picked.reshape(n_grp, n_seq), col), half)
    hot = (slots.reshape(n_experts)[:, None] == token_ids).astype(BF16)

    ring_lists = lax.dynamic_slice_in_dim(token_lists, grp * n_seq, n_seq, axis=0)
    ring_lists = jnp.concatenate([ring_lists, ring_lists], axis=0)
    ring_lists = lax.dynamic_slice_in_dim(ring_lists, col, n_seq, axis=0)
    pos, src_pos = ring_positions(ring_lists, tok_rows, n_grp, n_seq, col)

    full = tuple(up16(n_grp * k - n_grp // 2) for k in range(1, half + 1))
    usual = usual_caps(n_grp, n_seq)
    fits = lists_fit(token_lists, usual, tok_rows, n_grp, n_seq)
    fits = jnp.full((8, 128), fits, F32)
    n_rep = lax.axis_size("rep")
    agreed = fits
    for shift in range(1, n_rep):
        agreed = agreed * lax.ppermute(fits, "rep", [(i, (i + shift) % n_rep) for i in range(n_rep)])
    fin = lax.cond(
        agreed[0, 0] > 0.5,
        functools.partial(exchange, dims, usual, 0),
        functools.partial(exchange, dims, full, 1),
        tokens, token_cot, hot, pos, src_pos, w_gate[0], w_up[0], w_down[0],
    )
    fin = fin.reshape(n_experts, width + dims[3])

    gate_vals = jax.nn.sigmoid(router_logits)
    select = picked[None, :] == token_ids[:, None]
    own_gates = jnp.sum(jnp.where(select, gate_vals, 0.0), axis=0)
    gate_slots = to_slots(roll_columns(own_gates.reshape(n_grp, n_seq), col), half).reshape(n_experts)
    weight = jnp.where(slots.reshape(n_experts)[:, None] == token_ids, gate_slots[:, None], 0.0)
    token_grad = lax.dot_general(
        weight,
        fin[:, :width].astype(F32),
        (((0,), (0,)), ((), ())),
        precision=lax.Precision.HIGHEST,
        preferred_element_type=F32,
    )
    back_gates = from_slots(fin[:, width].reshape(2, n_grp, half), half)
    back_gates = roll_columns(back_gates, lax.rem(n_seq - col, n_seq)).reshape(n_experts).astype(F32)
    logit_grad = jnp.where(select, gate_vals * (1.0 - gate_vals) * back_gates[None, :], 0.0)
    return (token_grad.astype(BF16), logit_grad)


def solution(mesh):
    in_specs = (
        P(("rep", "grp", "seq"), None),
        P(("rep", "grp", "seq"), None),
        P(("rep", "grp", "seq"), None),
        P("rep", None),
        P(("grp", "seq"), None, None),
        P(("grp", "seq"), None, None),
        P(("grp", "seq"), None, None),
    )
    out_specs = (P(("rep", "grp", "seq"), None), P(("rep", "grp", "seq"), None))
    return jax.shard_map(body, mesh=mesh, in_specs=in_specs, out_specs=out_specs, check_vma=False)
```

```python
import functools
import math

import jax
import jax.numpy as jnp
from jax import lax
from jax.experimental import pallas as pl
from jax.experimental.pallas import tpu as pltpu
from jax.sharding import PartitionSpec as P

MESH = pl.DeviceIdType.MESH
BF16 = jnp.bfloat16
F32 = jnp.float32


def up16(n):
    return -(-n // 16) * 16


def usual_caps(n_grp, n_seq):
    total = n_grp * n_seq
    caps = []
    for k in range(1, n_seq // 2 + 1):
        slots = n_grp * k - n_grp // 2
        spread = math.sqrt(slots * (total - slots) / (4 * total))
        caps.append(-(-math.floor(min(slots, slots / 2 + 4.75 * spread)) // 8) * 8)
    return tuple(max(cap, caps[0]) for cap in caps)


def one_hot_rows(pos_row, rows):
    row_ids = lax.broadcasted_iota(jnp.int32, (rows, pos_row.shape[1]), 0)
    return jnp.where(row_ids == pos_row, 1.0, 0.0).astype(BF16)


def ring_kernel(dims, caps, ins, fin_ref, scratch):
    n_grp, n_seq, width, tail = dims
    half = n_seq // 2
    spc = half // 2
    wide = width + tail
    lanes = n_grp * half
    x_ref, g_ref, hot_ref, pos_ref, src_pos_ref, wg_hbm, wu_hbm, wd_hbm = ins
    packs, backs = scratch["packs"], (scratch["backs_a"], scratch["backs_b"])
    wg_ref, wu_ref, wd_ref = scratch["wg"], scratch["wu"], scratch["wd"]
    send_buf, own, fresh, final = scratch["send_buf"], scratch["own"], scratch["fresh"], scratch["final"]
    gate_scr, up_scr, dx = scratch["gate"], scratch["up"], (scratch["dx_a"], scratch["dx_b"])
    dropped, back_send = scratch["dropped"], scratch["back_send"]
    parts = ((0, width // 2), (width // 2, wide - width // 2))
    grp = lax.axis_index("grp")
    col = lax.axis_index("seq")
    cap_last = caps[half - 1]
    col_tile = min(width // 2, 512)
    n_tiles = width // col_tile

    def tile_cols(i):
        return pl.ds(pl.multiple_of(i * col_tile, col_tile), col_tile)

    def neighbour(direction):
        return lax.rem(col + 1 + direction * (n_seq - 2), n_seq)

    def peer(step):
        return lax.rem(grp + step, n_grp)

    weights = [
        pltpu.make_async_copy(wg_hbm, wg_ref, scratch["w_sem"].at[0]),
        pltpu.make_async_copy(wu_hbm, wu_ref, scratch["w_sem"].at[1]),
        pltpu.make_async_copy(wd_hbm, wd_ref, scratch["w_sem"].at[2]),
    ]

    barrier = pltpu.get_barrier_semaphore()
    for step in range(1, n_grp):
        pl.semaphore_signal(barrier, inc=1, device_id={"grp": peer(step)}, device_id_type=MESH)
    for direction in range(2):
        pl.semaphore_signal(barrier, inc=1, device_id={"seq": neighbour(direction)}, device_id_type=MESH)

    def pick(source, arr, chunk):
        hot = hot_ref[pl.ds(chunk * lanes, lanes), :]

        def tile(i, carry):
            cols = tile_cols(i)
            rows = jnp.dot(hot, source[:, cols], preferred_element_type=F32).astype(BF16)
            send_buf[arr, chunk, :, :, cols] = rows.reshape(n_grp, half, col_tile)
            return carry

        lax.fori_loop(0, n_tiles, tile, 0)

    def stage_copy(arr, chunk, step, src_grp):
        return pltpu.make_async_remote_copy(
            src_ref=send_buf.at[arr, chunk, peer(step)],
            dst_ref=own.at[arr, chunk, src_grp],
            send_sem=scratch["s1_send"].at[arr, chunk, step],
            recv_sem=scratch["s1_recv"].at[arr, chunk, step],
            device_id={"grp": peer(step)},
            device_id_type=MESH,
        )

    def stage_local(arr, chunk):
        return pltpu.make_async_copy(
            send_buf.at[arr, chunk, grp], own.at[arr, chunk, grp], scratch["loc_sem"].at[arr, chunk]
        )

    def stage_wait(arr, chunk):
        stage_local(arr, chunk).wait()
        for step in range(1, n_grp):
            stage_copy(arr, chunk, step, lax.rem(grp + n_grp - step, n_grp)).wait_recv()

    pick(x_ref, 0, 0)
    pl.semaphore_wait(barrier, n_grp + 1)
    for chunk, arr in ((0, 0), (0, 1), (1, 0), (1, 1)):
        if chunk or arr:
            pick((x_ref, g_ref)[arr], arr, chunk)
        stage_local(arr, chunk).start()
        for step in range(1, n_grp):
            stage_copy(arr, chunk, step, grp).start()
    for copy in weights:
        copy.start()

    def send_packet(step, arr, direction):
        if step + 1 < half:
            dst = packs[step + 1].at[arr, direction, pl.ds(0, caps[step])]
        else:
            dst = final.at[arr, pl.ds(direction * cap_last, cap_last)]
        return pltpu.make_async_remote_copy(
            src_ref=packs[step].at[arr, direction],
            dst_ref=dst,
            send_sem=scratch["d_send"].at[arr, direction, step],
            recv_sem=scratch["d_recv"].at[arr, direction, step],
            device_id={"seq": neighbour(direction)},
            device_id_type=MESH,
        )

    def make_fresh(step, arr):
        cap = caps[step]
        prev_cap = caps[step - 1] if step else 0

        def one(direction, carry):
            hot = one_hot_rows(pos_ref[pl.ds(2 * step + direction, 1), :], cap)

            def tile(i, inner):
                cols = tile_cols(i)
                mine = own[arr, step // spc, :, :, cols].reshape(lanes, col_tile)
                rows = jnp.dot(hot, mine, preferred_element_type=F32).astype(BF16)
                if prev_cap:
                    fresh[arr, direction, pl.ds(0, prev_cap), cols] = rows[:prev_cap]
                if cap > prev_cap:
                    packs[step][arr, direction, pl.ds(prev_cap, cap - prev_cap), cols] = rows[prev_cap:]
                return inner

            lax.fori_loop(0, n_tiles, tile, 0)
            return carry

        lax.fori_loop(0, 2, one, 0)

    for step in range(half):
        for arr in range(2):
            if step == 0:
                stage_wait(arr, 0)
                make_fresh(0, arr)

            def hop(direction, carry, step=step, arr=arr):
                if step:
                    prev = pl.ds(0, caps[step - 1])
                    send_packet(step - 1, arr, direction).wait_recv()
                    packs[step][arr, direction, prev, :] += fresh[arr, direction, prev, :]
                send_packet(step, arr, direction).start()
                return carry

            lax.fori_loop(0, 2, hop, 0)
            if step + 1 < half:
                if step + 1 == spc:
                    stage_wait(arr, 1)
                make_fresh(step + 1, arr)

    same_hot = one_hot_rows(pos_ref[pl.ds(2 * half, 1), :], 16)
    for arr in range(2):

        def same_tile(i, inner, arr=arr):
            cols = tile_cols(i)
            mine = own[arr, 0, :, :, cols].reshape(lanes, col_tile)
            rows = jnp.dot(same_hot, mine, preferred_element_type=F32)
            final[arr, pl.ds(2 * cap_last, 16), cols] = rows.astype(BF16)
            return inner

        lax.fori_loop(0, n_tiles, same_tile, 0)

    for copy in weights:
        copy.wait()
    for direction in range(2):
        send_packet(half - 1, 0, direction).wait_recv()
    gate_scr[...] = jnp.dot(final[0], wg_ref[...], preferred_element_type=F32)
    up_scr[...] = jnp.dot(final[0], wu_ref[...], preferred_element_type=F32)
    for direction in range(2):
        send_packet(half - 1, 1, direction).wait_recv()
    nt = (((1,), (1,)), ((), ()))
    d_hidden = lax.dot_general(final[1], wd_ref[...], nt, preferred_element_type=F32)
    gate_pre = gate_scr[...]
    up_pre = up_scr[...]
    sig = jax.nn.sigmoid(gate_pre)
    activated = gate_pre * sig
    hidden = (activated * up_pre).astype(BF16).astype(F32)
    gate_grad = jnp.sum(hidden * d_hidden, axis=1, keepdims=True)
    scratch["d_gate"][...] = (d_hidden * up_pre * sig * (1.0 + gate_pre * (1.0 - sig))).astype(BF16)
    scratch["d_up"][...] = (d_hidden * activated).astype(BF16)
    dx[1][:, width // 2 :] = jnp.broadcast_to(gate_grad, (gate_grad.shape[0], tail)).astype(BF16)

    def send_back(step, part, direction):
        cap = caps[half - 1 - step]
        if step == 0:
            src = dx[part].at[pl.ds(direction * cap_last, cap_last)]
        else:
            src = backs[part][step - 1].at[direction, pl.ds(0, cap)]
        return pltpu.make_async_remote_copy(
            src_ref=src,
            dst_ref=backs[part][step].at[direction],
            send_sem=scratch["r_send"].at[part, direction, step],
            recv_sem=scratch["r_recv"].at[part, direction, step],
            device_id={"seq": neighbour(1 - direction)},
            device_id_type=MESH,
        )

    for part in range(2):

        def dx_tile(i, carry, part=part):
            w_rows = tile_cols(i + part * (n_tiles // 2))
            rows = lax.dot_general(scratch["d_gate"][...], wg_ref[w_rows, :], nt, preferred_element_type=F32)
            rows = rows + lax.dot_general(scratch["d_up"][...], wu_ref[w_rows, :], nt, preferred_element_type=F32)
            dx[part][:, tile_cols(i)] = rows.astype(BF16)
            return carry

        lax.fori_loop(0, n_tiles // 2, dx_tile, 0)
        for direction in range(2):
            send_back(0, part, direction).start()

    def home_copy(chunk, step, src_grp):
        return pltpu.make_async_remote_copy(
            src_ref=back_send.at[chunk, peer(step)],
            dst_ref=fin_ref.at[chunk, src_grp],
            send_sem=scratch["s2_send"].at[chunk, step],
            recv_sem=scratch["s2_recv"].at[chunk, step],
            device_id={"grp": peer(step)},
            device_id_type=MESH,
        )

    def home_local(chunk):
        return pltpu.make_async_copy(back_send.at[chunk, grp], fin_ref.at[chunk, grp], scratch["loc_sem"].at[2, chunk])

    tn = (((0,), (0,)), ((), ()))

    def drop(row, cap, rows, slot, part, add=False):
        hot = one_hot_rows(src_pos_ref[pl.ds(row, 1), :n_grp], cap)
        first, size = parts[part]
        kept = lax.dot_general(hot, rows, tn, preferred_element_type=F32)
        at = pl.ds(slot * n_grp, n_grp)
        if add:
            kept = kept + dropped[at, pl.ds(first, size)]
        dropped[at, pl.ds(first, size)] = kept

    def regroup(chunk):
        shape = (lanes, lanes)
        to = lax.broadcasted_iota(jnp.int32, shape, 0)
        frm = lax.broadcasted_iota(jnp.int32, shape, 1)
        perm = jnp.where((to // half == frm % n_grp) & (to % half == frm // n_grp), 1.0, 0.0).astype(BF16)

        def put(cols, size):
            rows = jnp.dot(perm, dropped[:, cols].astype(BF16), preferred_element_type=F32).astype(BF16)
            back_send[chunk, :, :, cols] = rows.reshape(n_grp, half, size)

        def tile(i, carry):
            put(tile_cols(i), col_tile)
            return carry

        lax.fori_loop(0, n_tiles, tile, 0)
        put(pl.ds(width, tail), tail)

    for step in range(half):
        chunk = 1 if step < spc else 0
        k = half - 1 - step
        for part in range(2):
            for direction in range(2):
                send_back(step, part, direction).wait_recv()
                if step + 1 < half:
                    send_back(step + 1, part, direction).start()
            if step == spc:
                drop(2 * half, 16, dx[part][pl.ds(2 * cap_last, 16), :], spc, part)
            for direction in range(2):
                slot = k % spc + (spc if direction and k else 0)
                drop(2 * k + direction, caps[k], backs[part][step][direction], slot, part, bool(direction and k == 0))
        if step in (spc - 1, half - 1):
            regroup(chunk)
            home_local(chunk).start()
            for s in range(1, n_grp):
                home_copy(chunk, s, grp).start()

    for arr in range(2):
        for chunk in range(2):
            for s in range(1, n_grp):
                stage_copy(arr, chunk, s, grp).wait_send()
    for step in range(half):
        for direction in range(2):
            for arr in range(2):
                send_packet(step, arr, direction).wait_send()
                send_back(step, arr, direction).wait_send()
    for chunk in (1, 0):
        home_local(chunk).wait()
        for s in range(1, n_grp):
            home_copy(chunk, s, grp).wait_send()
            home_copy(chunk, s, lax.rem(grp + n_grp - s, n_grp)).wait_recv()


N_INS = 8


def exchange(dims, caps, collective_id, *operands):
    n_grp, n_seq, width, tail = dims
    half = n_seq // 2
    w_gate, w_up, w_down = operands[5:]
    ff = w_gate.shape[1]
    wide = width + tail
    rows = 2 * caps[-1] + 16
    lanes = n_grp * half
    dma = pltpu.SemaphoreType.DMA
    vmem = pl.BlockSpec(memory_space=pltpu.VMEM)
    hbm = pl.BlockSpec(memory_space=pl.ANY)
    scratch = {
        "wg": pltpu.VMEM(w_gate.shape, BF16),
        "wu": pltpu.VMEM(w_up.shape, BF16),
        "wd": pltpu.VMEM(w_down.shape, BF16),
        "send_buf": pltpu.VMEM((2, 2, n_grp, half, width), BF16),
        "own": pltpu.VMEM((2, 2, n_grp, half, width), BF16),
        "packs": [pltpu.VMEM((2, 2, cap, width), BF16) for cap in caps],
        "fresh": pltpu.VMEM((2, 2, caps[-2], width), BF16),
        "final": pltpu.VMEM((2, rows, width), BF16),
        "gate": pltpu.VMEM((rows, ff), F32),
        "up": pltpu.VMEM((rows, ff), F32),
        "d_gate": pltpu.VMEM((rows, ff), BF16),
        "d_up": pltpu.VMEM((rows, ff), BF16),
        "dx_a": pltpu.VMEM((rows, width // 2), BF16),
        "dx_b": pltpu.VMEM((rows, wide - width // 2), BF16),
        "backs_a": [pltpu.VMEM((2, cap, width // 2), BF16) for cap in reversed(caps)],
        "backs_b": [pltpu.VMEM((2, cap, wide - width // 2), BF16) for cap in reversed(caps)],
        "dropped": pltpu.VMEM((lanes, wide), F32),
        "back_send": pltpu.VMEM((2, n_grp, half, wide), BF16),
        "w_sem": dma((3,)),
        "s1_send": dma((2, 2, n_grp)),
        "s1_recv": dma((2, 2, n_grp)),
        "d_send": dma((2, 2, half)),
        "d_recv": dma((2, 2, half)),
        "r_send": dma((2, 2, half)),
        "r_recv": dma((2, 2, half)),
        "s2_send": dma((2, n_grp)),
        "s2_recv": dma((2, n_grp)),
        "loc_sem": dma((3, 2)),
    }
    leaves, tree = jax.tree.flatten(scratch, is_leaf=lambda leaf: not isinstance(leaf, (dict, list)))

    def kernel(*refs):
        named = jax.tree.unflatten(tree, refs[N_INS + 1 :])
        ring_kernel(dims, caps, refs[:N_INS], refs[N_INS], named)

    return pl.pallas_call(
        kernel,
        out_shape=jax.ShapeDtypeStruct((2, n_grp, half, wide), BF16),
        in_specs=[vmem] * 5 + [hbm] * 3,
        out_specs=vmem,
        scratch_shapes=leaves,
        compiler_params=pltpu.CompilerParams(
            collective_id=collective_id, has_side_effects=True, vmem_limit_bytes=60 * 1024 * 1024
        ),
        name=f"ring_exchange_{collective_id}",
    )(*operands)


def to_slots(values, half):
    spc = half // 2
    first = jnp.concatenate(
        [jnp.flip(values[:, spc + 1 : half + 1], 1), values[:, :1], values[:, half + 1 : half + spc]], axis=1
    )
    second = jnp.concatenate([jnp.flip(values[:, 1 : spc + 1], 1), values[:, half + spc :]], axis=1)
    return jnp.stack([first, second])


def from_slots(slots, half):
    spc = half // 2
    first, second = slots[0], slots[1]
    return jnp.concatenate(
        [
            first[:, spc : spc + 1],
            jnp.flip(second[:, :spc], 1),
            jnp.flip(first[:, :spc], 1),
            first[:, spc + 1 :],
            second[:, spc:],
        ],
        axis=1,
    )


def roll_columns(values, start):
    doubled = jnp.concatenate([values, values], axis=1)
    return lax.dynamic_slice_in_dim(doubled, start, values.shape[1], axis=1)


def prepare_kernel(dims, tok_rows, caps, lists_ref, flag_ref, picked_ref, hot_ref, pos_ref, src_pos_ref, got, send_sem, recv_sem):
    n_grp, n_seq, n_rep = dims
    half = n_seq // 2
    spc = half // 2
    lanes = n_grp * half
    n_experts = lists_ref.shape[0]
    rep, grp, col = lax.axis_index("rep"), lax.axis_index("grp"), lax.axis_index("seq")
    me = grp * n_seq + col

    def peer(step):
        return lax.rem(rep + step, n_rep)

    barrier = pltpu.get_barrier_semaphore()
    for step in range(1, n_rep):
        pl.semaphore_signal(barrier, inc=1, device_id={"rep": peer(step)}, device_id_type=MESH)

    def iota(shape, axis):
        return lax.broadcasted_iota(jnp.int32, shape, axis)

    def shift(n):
        return n.bit_length() - 1

    lists = jnp.transpose(lists_ref[...])
    owner = lists >> shift(tok_rows)
    src = owner >> shift(n_seq)
    column = owner & (n_seq - 1)
    expert = iota((1, n_experts), 1)
    dest = expert & (n_seq - 1)
    low = src < n_grp // 2
    gap_up = (dest - column) & (n_seq - 1)
    gap_down = (column - dest) & (n_seq - 1)
    d_up = jnp.where((gap_up < half) | ((gap_up == half) & low), gap_up, 0)
    d_down = jnp.where((gap_down < half) | ((gap_down == half) & ~low), gap_down, 0)

    def count(mask):
        return jnp.sum(mask.astype(jnp.int32), axis=0, keepdims=True)

    over = jnp.zeros((1, n_experts), jnp.int32)
    for k, cap in enumerate(caps):
        if cap < n_grp * (k + 1) - n_grp // 2:
            for distance in (d_up, d_down):
                over = jnp.maximum(over, count(distance >= half - k) - cap)
    bad = jnp.max(over.astype(F32), axis=1, keepdims=True)
    got[0] = jnp.broadcast_to(jnp.where(bad > 0.5, 0.0, 1.0), got.shape[1:])
    pl.semaphore_wait(barrier, n_rep - 1)

    def tell(step):
        return pltpu.make_async_remote_copy(
            src_ref=got.at[0],
            dst_ref=got.at[step],
            send_sem=send_sem.at[step],
            recv_sem=recv_sem.at[step],
            device_id={"rep": peer(step)},
            device_id_type=MESH,
        )

    for step in range(1, n_rep):
        tell(step).start()

    local = lists - me * tok_rows
    mine = (local >= 0) & (local < tok_rows)
    picked = jnp.max(jnp.where(mine, local, -1), axis=0, keepdims=True)
    picked_ref[...] = jnp.broadcast_to(picked, picked_ref.shape)

    shape = (n_experts, n_experts)
    row = iota(shape, 0)
    turn = row & (spc - 1)
    chunk = row >> shift(lanes)
    distance = half - spc * chunk - turn
    backward = (row >> shift(spc)) & 1
    rel = jnp.where(backward == 0, distance, jnp.where(distance == half, 0, n_seq - distance))
    wanted = ((row >> shift(half)) & (n_grp - 1)) * n_seq + ((rel + col) & (n_seq - 1))
    perm = jnp.where(iota(shape, 1) == wanted, 1.0, 0.0).astype(BF16)
    hot_t = jnp.where(iota((tok_rows, n_experts), 0) == picked, 1.0, 0.0).astype(BF16)
    nt = (((1,), (1,)), ((), ()))
    hot_ref[...] = lax.dot_general(perm, hot_t, nt, preferred_element_type=F32).astype(BF16)

    here = column == col
    up_gap = (dest - col) & (n_seq - 1)
    down_gap = (col - dest) & (n_seq - 1)
    ahead_up = count(d_up > up_gap)
    ahead_down = count(d_down > down_gap)
    source = iota((n_grp, n_experts), 0)
    rows_up = jnp.zeros((n_grp, n_experts), jnp.int32)
    rows_down, rows_same = rows_up, rows_up
    for g in range(n_grp):
        present = count(here & (src == g))
        goes_up = (up_gap < half) | (up_gap == half) if g < n_grp // 2 else up_gap < half
        goes_down = down_gap < half if g < n_grp // 2 else (down_gap < half) | (down_gap == half)
        at_up = jnp.where(goes_up, present, 0)
        at_down = jnp.where(goes_down, present, 0)
        ahead_up = ahead_up + at_up
        ahead_down = ahead_down + at_down
        rows_up = jnp.where(source == g, at_up * ahead_up, rows_up)
        rows_down = jnp.where(source == g, at_down * ahead_down, rows_down)
        rows_same = jnp.where(source == g, present * (g + 1), rows_same)

    n_rows = src_pos_ref.shape[0]
    shape = (n_rows, n_experts)
    row = iota(shape, 0)
    hop = half - (row >> 1)
    lane = iota(shape, 1)
    base = grp * n_seq

    def pick(offset, on):
        wanted = base + ((col + offset) & (n_seq - 1))
        return jnp.where((lane == wanted) & on, 1.0, 0.0).astype(BF16)

    def take(select, values):
        return lax.dot_general(select, values.astype(F32).astype(BF16), nt, preferred_element_type=F32)

    stepping = row < n_seq
    places = take(pick(hop, stepping & ((row & 1) == 0)), rows_up)
    places = places + take(pick(n_seq - hop, stepping & ((row & 1) == 1)), rows_down)
    places = places + take(pick(0, row == n_seq), rows_same)
    src_pos_ref[...] = places.astype(jnp.int32) - 1
    shape = (n_grp, lanes)
    spread = jnp.where(iota(shape, 1) >> shift(half) == iota(shape, 0), 1.0, 0.0).astype(BF16)
    wide = jnp.dot(places.astype(BF16), spread, preferred_element_type=F32).astype(jnp.int32)
    shape = (n_rows, lanes)
    row = iota(shape, 0)
    slot = ((row >> 1) & (spc - 1)) + spc * (row & 1)
    slot = jnp.where(row == 1, 0, jnp.where(row == n_seq, spc, slot))
    pos_ref[...] = jnp.where((iota(shape, 1) & (half - 1)) == slot, wide, 0) - 1

    for step in range(1, n_rep):
        tell(step).wait()
    flag = got[0]
    for step in range(1, n_rep):
        flag = flag * got[step]
    flag_ref[...] = flag


def prepare(dims, tok_rows, caps, lists):
    n_grp, n_seq, n_rep = dims
    n_experts = lists.shape[0]
    n_rows = n_seq + 8
    lanes = n_grp * (n_seq // 2)
    vmem = pl.BlockSpec(memory_space=pltpu.VMEM)
    return pl.pallas_call(
        functools.partial(prepare_kernel, dims, tok_rows, caps),
        out_shape=(
            jax.ShapeDtypeStruct((8, 128), F32),
            jax.ShapeDtypeStruct((8, n_experts), jnp.int32),
            jax.ShapeDtypeStruct((n_experts, tok_rows), BF16),
            jax.ShapeDtypeStruct((n_rows, lanes), jnp.int32),
            jax.ShapeDtypeStruct((n_rows, n_grp), jnp.int32),
        ),
        in_specs=[vmem],
        out_specs=(vmem,) * 5,
        scratch_shapes=[
            pltpu.VMEM((n_rep, 8, 128), F32),
            pltpu.SemaphoreType.DMA((n_rep,)),
            pltpu.SemaphoreType.DMA((n_rep,)),
        ],
        compiler_params=pltpu.CompilerParams(
            collective_id=2, has_side_effects=True, vmem_limit_bytes=16 * 1024 * 1024
        ),
        name="prepare",
    )(lists)


def body(tokens, token_cot, router_logits, token_lists, w_gate, w_up, w_down):
    n_grp = lax.axis_size("grp")
    n_seq = lax.axis_size("seq")
    half = n_seq // 2
    col = lax.axis_index("seq")
    tok_rows, width = tokens.shape
    n_experts, cap = token_lists.shape
    dims = (n_grp, n_seq, width, 128)

    token_ids = jnp.arange(tok_rows, dtype=jnp.int32)
    full = tuple(up16(n_grp * k - n_grp // 2) for k in range(1, half + 1))
    usual = usual_caps(n_grp, n_seq)
    flag, picked, hot, pos, src_pos = prepare((n_grp, n_seq, lax.axis_size("rep")), tok_rows, usual, token_lists)
    picked = picked[0]
    fin = lax.cond(
        flag[0, 0] > 0.5,
        functools.partial(exchange, dims, usual, 0),
        functools.partial(exchange, dims, full, 1),
        tokens, token_cot, hot, pos, src_pos, w_gate[0], w_up[0], w_down[0],
    )
    fin = fin.reshape(n_experts, width + dims[3])

    gate_vals = jax.nn.sigmoid(router_logits)
    select = picked[None, :] == token_ids[:, None]
    own_gates = jnp.sum(jnp.where(select, gate_vals, 0.0), axis=0)
    gate_slots = to_slots(roll_columns(own_gates.reshape(n_grp, n_seq), col), half).reshape(n_experts)
    weight = hot.astype(F32) * gate_slots[:, None]
    token_grad = lax.dot_general(
        weight,
        fin[:, :width].astype(F32),
        (((0,), (0,)), ((), ())),
        precision=lax.Precision.HIGHEST,
        preferred_element_type=F32,
    )
    back_gates = from_slots(fin[:, width].reshape(2, n_grp, half), half)
    back_gates = roll_columns(back_gates, lax.rem(n_seq - col, n_seq)).reshape(n_experts).astype(F32)
    logit_grad = jnp.where(select, gate_vals * (1.0 - gate_vals) * back_gates[None, :], 0.0)
    return (token_grad.astype(BF16), logit_grad)


def solution(mesh):
    in_specs = (
        P(("rep", "grp", "seq"), None),
        P(("rep", "grp", "seq"), None),
        P(("rep", "grp", "seq"), None),
        P("rep", None),
        P(("grp", "seq"), None, None),
        P(("grp", "seq"), None, None),
        P(("grp", "seq"), None, None),
    )
    out_specs = (P(("rep", "grp", "seq"), None), P(("rep", "grp", "seq"), None))
    return jax.shard_map(body, mesh=mesh, in_specs=in_specs, out_specs=out_specs, check_vma=False)
```

```python
import functools
import math

import jax
import jax.numpy as jnp
from jax import lax
from jax.experimental import pallas as pl
from jax.experimental.pallas import tpu as pltpu
from jax.sharding import PartitionSpec as P

MESH = pl.DeviceIdType.MESH
BF16 = jnp.bfloat16
F32 = jnp.float32
CHUNKS = 4
GRAIN = 4


def to_grain(n):
    return -(-n // GRAIN) * GRAIN


def usual_caps(n_grp, n_seq):
    total = n_grp * n_seq
    caps = []
    for k in range(1, n_seq // 2 + 1):
        slots = n_grp * k - n_grp // 2
        spread = math.sqrt(slots * (total - slots) / (4 * total))
        caps.append(-(-math.floor(min(slots, slots / 2 + 4.75 * spread)) // GRAIN) * GRAIN)
    return tuple(max(cap, caps[0]) for cap in caps)


def one_hot_rows(pos_row, rows):
    row_ids = lax.broadcasted_iota(jnp.int32, (rows, pos_row.shape[1]), 0)
    return jnp.where(row_ids == pos_row, 1.0, 0.0).astype(BF16)


def ring_kernel(dims, caps, ins, fin_ref, scratch):
    n_grp, n_seq, width, tail = dims
    half = n_seq // 2
    spc = half // CHUNKS
    slots = 2 * spc
    wide = width + tail
    lanes = n_grp * slots
    x_ref, g_ref, hot_ref, pos_ref, src_pos_ref, wg_hbm, wu_hbm, wd_hbm = ins
    packs, backs = scratch["packs"], (scratch["backs_a"], scratch["backs_b"])
    wg_ref, wu_ref, wd_ref = scratch["wg"], scratch["wu"], scratch["wd"]
    send_buf, own, fresh, final, flat = (scratch[name] for name in ("send_buf", "own", "fresh", "final", "flat"))
    gate_scr, up_scr, dx = scratch["gate"], scratch["up"], (scratch["dx_a"], scratch["dx_b"])
    dropped, back_send = scratch["dropped"], scratch["back_send"]
    parts = ((0, width // 2), (width // 2, wide - width // 2))
    grp = lax.axis_index("grp")
    col = lax.axis_index("seq")
    cap_last = caps[half - 1]
    col_tile = min(width // 2, 512)
    n_tiles = width // col_tile

    def tile_cols(i):
        return pl.ds(pl.multiple_of(i * col_tile, col_tile), col_tile)

    def neighbour(direction):
        return lax.rem(col + 1 + direction * (n_seq - 2), n_seq)

    def peer(step):
        return lax.rem(grp + step, n_grp)

    weights = [
        pltpu.make_async_copy(wg_hbm, wg_ref, scratch["w_sem"].at[0]),
        pltpu.make_async_copy(wu_hbm, wu_ref, scratch["w_sem"].at[1]),
        pltpu.make_async_copy(wd_hbm, wd_ref, scratch["w_sem"].at[2]),
    ]

    barrier = pltpu.get_barrier_semaphore()
    for step in range(1, n_grp):
        pl.semaphore_signal(barrier, inc=1, device_id={"grp": peer(step)}, device_id_type=MESH)
    for direction in range(2):
        pl.semaphore_signal(barrier, inc=1, device_id={"seq": neighbour(direction)}, device_id_type=MESH)

    def pick(source, arr, chunk):
        hot = hot_ref[pl.ds(chunk * lanes, lanes), :]

        def tile(i, carry):
            cols = tile_cols(i)
            rows = jnp.dot(hot, source[:, cols], preferred_element_type=F32).astype(BF16)
            send_buf[arr, chunk, :, :, cols] = rows.reshape(n_grp, slots, col_tile)
            return carry

        lax.fori_loop(0, n_tiles, tile, 0)

    def stage_copy(arr, chunk, step, src_grp):
        return pltpu.make_async_remote_copy(
            src_ref=send_buf.at[arr, chunk, peer(step)],
            dst_ref=own.at[arr, chunk, src_grp],
            send_sem=scratch["s1_send"].at[arr, chunk, step],
            recv_sem=scratch["s1_recv"].at[arr, chunk, step],
            device_id={"grp": peer(step)},
            device_id_type=MESH,
        )

    def stage_local(arr, chunk):
        return pltpu.make_async_copy(
            send_buf.at[arr, chunk, grp], own.at[arr, chunk, grp], scratch["loc_sem"].at[arr, chunk]
        )

    def stage_wait(arr, chunk):
        stage_local(arr, chunk).wait()
        for step in range(1, n_grp):
            stage_copy(arr, chunk, step, lax.rem(grp + n_grp - step, n_grp)).wait_recv()

    pick(x_ref, 0, 0)
    pl.semaphore_wait(barrier, n_grp + 1)
    for chunk, arr in [(chunk, arr) for chunk in range(CHUNKS) for arr in range(2)]:
        if chunk or arr:
            pick((x_ref, g_ref)[arr], arr, chunk)
        stage_local(arr, chunk).start()
        for step in range(1, n_grp):
            stage_copy(arr, chunk, step, grp).start()
    for copy in weights:
        copy.start()

    def send_packet(step, arr, direction):
        if step + 1 < half:
            dst = packs[step + 1].at[arr, direction, pl.ds(0, caps[step] // GRAIN)]
        else:
            dst = final.at[arr, pl.ds(direction * cap_last // GRAIN, cap_last // GRAIN)]
        return pltpu.make_async_remote_copy(
            src_ref=packs[step].at[arr, direction],
            dst_ref=dst,
            send_sem=scratch["d_send"].at[arr, direction, step],
            recv_sem=scratch["d_recv"].at[arr, direction, step],
            device_id={"seq": neighbour(direction)},
            device_id_type=MESH,
        )

    def make_fresh(step, arr):
        cap = caps[step]
        prev_cap = caps[step - 1] if step else 0

        def one(direction, carry):
            hot = one_hot_rows(pos_ref[pl.ds(2 * step + direction, 1), :], cap)

            def tile(i, inner):
                cols = tile_cols(i)
                mine = own[arr, step // spc, :, :, cols].reshape(lanes, col_tile)
                rows = jnp.dot(hot, mine, preferred_element_type=F32).astype(BF16)
                rows = rows.reshape(cap // GRAIN, GRAIN, col_tile)
                held = prev_cap // GRAIN
                if held:
                    fresh[arr, direction, pl.ds(0, held), :, cols] = rows[:held]
                if cap > prev_cap:
                    packs[step][arr, direction, pl.ds(held, cap // GRAIN - held), :, cols] = rows[held:]
                return inner

            lax.fori_loop(0, n_tiles, tile, 0)
            return carry

        lax.fori_loop(0, 2, one, 0)

    for step in range(half):
        for arr in range(2):
            if step == 0:
                stage_wait(arr, 0)
                make_fresh(0, arr)

            def hop(direction, carry, step=step, arr=arr):
                if step:
                    prev = pl.ds(0, caps[step - 1] // GRAIN)
                    send_packet(step - 1, arr, direction).wait_recv()
                    packs[step][arr, direction, prev] += fresh[arr, direction, prev]
                send_packet(step, arr, direction).start()
                return carry

            lax.fori_loop(0, 2, hop, 0)
            if step + 1 < half:
                if (step + 1) % spc == 0:
                    stage_wait(arr, (step + 1) // spc)
                make_fresh(step + 1, arr)

    same_hot = one_hot_rows(pos_ref[pl.ds(2 * half, 1), :], 16)
    for arr in range(2):

        def same_tile(i, inner, arr=arr):
            cols = tile_cols(i)
            mine = own[arr, 0, :, :, cols].reshape(lanes, col_tile)
            rows = jnp.dot(same_hot, mine, preferred_element_type=F32)
            flat[arr, pl.ds(2 * cap_last, 16), cols] = rows.astype(BF16)
            return inner

        lax.fori_loop(0, n_tiles, same_tile, 0)

    for copy in weights:
        copy.wait()
    def take_packets(arr):
        for direction in range(2):
            send_packet(half - 1, arr, direction).wait_recv()

        def tile(i, carry):
            cols = tile_cols(i)
            flat[arr, pl.ds(0, 2 * cap_last), cols] = final[arr, :, :, cols].reshape(2 * cap_last, col_tile)
            return carry

        lax.fori_loop(0, n_tiles, tile, 0)

    take_packets(0)
    gate_scr[...] = jnp.dot(flat[0], wg_ref[...], preferred_element_type=F32)
    up_scr[...] = jnp.dot(flat[0], wu_ref[...], preferred_element_type=F32)
    take_packets(1)
    nt = (((1,), (1,)), ((), ()))
    d_hidden = lax.dot_general(flat[1], wd_ref[...], nt, preferred_element_type=F32)
    gate_pre = gate_scr[...]
    up_pre = up_scr[...]
    sig = jax.nn.sigmoid(gate_pre)
    activated = gate_pre * sig
    hidden = (activated * up_pre).astype(BF16).astype(F32)
    gate_grad = jnp.sum(hidden * d_hidden, axis=1, keepdims=True)
    scratch["d_gate"][...] = (d_hidden * up_pre * sig * (1.0 + gate_pre * (1.0 - sig))).astype(BF16)
    scratch["d_up"][...] = (d_hidden * activated).astype(BF16)
    n_rows = gate_grad.shape[0]
    gates = jnp.broadcast_to(gate_grad, (n_rows, tail)).astype(BF16)
    dx[1][:, :, width // 2 :] = gates.reshape(n_rows // GRAIN, GRAIN, tail)

    def send_back(step, part, direction):
        cap = caps[half - 1 - step]
        if step == 0:
            src = dx[part].at[pl.ds(direction * cap_last // GRAIN, cap_last // GRAIN)]
        else:
            src = backs[part][step - 1].at[direction, pl.ds(0, cap // GRAIN)]
        return pltpu.make_async_remote_copy(
            src_ref=src,
            dst_ref=backs[part][step].at[direction],
            send_sem=scratch["r_send"].at[part, direction, step],
            recv_sem=scratch["r_recv"].at[part, direction, step],
            device_id={"seq": neighbour(1 - direction)},
            device_id_type=MESH,
        )

    for part in range(2):

        def dx_tile(i, carry, part=part):
            w_rows = tile_cols(i + part * (n_tiles // 2))
            rows = lax.dot_general(scratch["d_gate"][...], wg_ref[w_rows, :], nt, preferred_element_type=F32)
            rows = rows + lax.dot_general(scratch["d_up"][...], wu_ref[w_rows, :], nt, preferred_element_type=F32)
            dx[part][:, :, tile_cols(i)] = rows.astype(BF16).reshape(n_rows // GRAIN, GRAIN, col_tile)
            return carry

        lax.fori_loop(0, n_tiles // 2, dx_tile, 0)
        for direction in range(2):
            send_back(0, part, direction).start()

    def home_copy(chunk, step, src_grp):
        return pltpu.make_async_remote_copy(
            src_ref=back_send.at[chunk, peer(step)],
            dst_ref=fin_ref.at[chunk, src_grp],
            send_sem=scratch["s2_send"].at[chunk, step],
            recv_sem=scratch["s2_recv"].at[chunk, step],
            device_id={"grp": peer(step)},
            device_id_type=MESH,
        )

    def home_local(chunk):
        return pltpu.make_async_copy(back_send.at[chunk, grp], fin_ref.at[chunk, grp], scratch["loc_sem"].at[2, chunk])

    tn = (((0,), (0,)), ((), ()))

    def drop(row, cap, rows, slot, part, add=False):
        hot = one_hot_rows(src_pos_ref[pl.ds(row, 1), :n_grp], cap)
        first, size = parts[part]
        kept = lax.dot_general(hot, rows.reshape(cap, size), tn, preferred_element_type=F32)
        at = pl.ds(slot * n_grp, n_grp)
        if add:
            kept = kept + dropped[at, pl.ds(first, size)]
        dropped[at, pl.ds(first, size)] = kept

    def regroup(chunk):
        shape = (lanes, lanes)
        to = lax.broadcasted_iota(jnp.int32, shape, 0)
        frm = lax.broadcasted_iota(jnp.int32, shape, 1)
        perm = jnp.where((to // slots == frm % n_grp) & (to % slots == frm // n_grp), 1.0, 0.0).astype(BF16)

        def put(cols, size):
            rows = jnp.dot(perm, dropped[:, cols].astype(BF16), preferred_element_type=F32).astype(BF16)
            back_send[chunk, :, :, cols] = rows.reshape(n_grp, slots, size)

        def tile(i, carry):
            put(tile_cols(i), col_tile)
            return carry

        lax.fori_loop(0, n_tiles, tile, 0)
        put(pl.ds(width, tail), tail)

    for step in range(half):
        k = half - 1 - step
        chunk = k // spc
        for part in range(2):
            for direction in range(2):
                send_back(step, part, direction).wait_recv()
                if step + 1 < half:
                    send_back(step + 1, part, direction).start()
            if k == spc - 1:
                drop(2 * half, 16, dx[part][pl.ds(2 * cap_last // GRAIN, 16 // GRAIN)], spc, part)
            for direction in range(2):
                slot = k % spc + (spc if direction and k else 0)
                drop(2 * k + direction, caps[k], backs[part][step][direction], slot, part, bool(direction and k == 0))
        if k % spc == 0:
            regroup(chunk)
            home_local(chunk).start()
            for s in range(1, n_grp):
                home_copy(chunk, s, grp).start()

    for arr in range(2):
        for chunk in range(CHUNKS):
            for s in range(1, n_grp):
                stage_copy(arr, chunk, s, grp).wait_send()
    for step in range(half):
        for direction in range(2):
            for arr in range(2):
                send_packet(step, arr, direction).wait_send()
                send_back(step, arr, direction).wait_send()
    for chunk in reversed(range(CHUNKS)):
        home_local(chunk).wait()
        for s in range(1, n_grp):
            home_copy(chunk, s, grp).wait_send()
            home_copy(chunk, s, lax.rem(grp + n_grp - s, n_grp)).wait_recv()


N_INS = 8


def exchange(dims, caps, collective_id, *operands):
    n_grp, n_seq, width, tail = dims
    half = n_seq // 2
    w_gate, w_up, w_down = operands[5:]
    ff = w_gate.shape[1]
    wide = width + tail
    rows = 2 * caps[-1] + 16
    slots = 2 * (half // CHUNKS)
    lanes = n_grp * slots
    dma = pltpu.SemaphoreType.DMA
    vmem = pl.BlockSpec(memory_space=pltpu.VMEM)
    hbm = pl.BlockSpec(memory_space=pl.ANY)
    scratch = {
        "wg": pltpu.VMEM(w_gate.shape, BF16),
        "wu": pltpu.VMEM(w_up.shape, BF16),
        "wd": pltpu.VMEM(w_down.shape, BF16),
        "send_buf": pltpu.VMEM((2, CHUNKS, n_grp, slots, width), BF16),
        "own": pltpu.VMEM((2, CHUNKS, n_grp, slots, width), BF16),
        "packs": [pltpu.VMEM((2, 2, cap // GRAIN, GRAIN, width), BF16) for cap in caps],
        "fresh": pltpu.VMEM((2, 2, caps[-2] // GRAIN, GRAIN, width), BF16),
        "final": pltpu.VMEM((2, 2 * caps[-1] // GRAIN, GRAIN, width), BF16),
        "flat": pltpu.VMEM((2, rows, width), BF16),
        "gate": pltpu.VMEM((rows, ff), F32),
        "up": pltpu.VMEM((rows, ff), F32),
        "d_gate": pltpu.VMEM((rows, ff), BF16),
        "d_up": pltpu.VMEM((rows, ff), BF16),
        "dx_a": pltpu.VMEM((rows // GRAIN, GRAIN, width // 2), BF16),
        "dx_b": pltpu.VMEM((rows // GRAIN, GRAIN, wide - width // 2), BF16),
        "backs_a": [pltpu.VMEM((2, cap // GRAIN, GRAIN, width // 2), BF16) for cap in reversed(caps)],
        "backs_b": [pltpu.VMEM((2, cap // GRAIN, GRAIN, wide - width // 2), BF16) for cap in reversed(caps)],
        "dropped": pltpu.VMEM((lanes, wide), F32),
        "back_send": pltpu.VMEM((CHUNKS, n_grp, slots, wide), BF16),
        "w_sem": dma((3,)),
        "s1_send": dma((2, CHUNKS, n_grp)),
        "s1_recv": dma((2, CHUNKS, n_grp)),
        "d_send": dma((2, 2, half)),
        "d_recv": dma((2, 2, half)),
        "r_send": dma((2, 2, half)),
        "r_recv": dma((2, 2, half)),
        "s2_send": dma((CHUNKS, n_grp)),
        "s2_recv": dma((CHUNKS, n_grp)),
        "loc_sem": dma((3, CHUNKS)),
    }
    leaves, tree = jax.tree.flatten(scratch, is_leaf=lambda leaf: not isinstance(leaf, (dict, list)))

    def kernel(*refs):
        named = jax.tree.unflatten(tree, refs[N_INS + 1 :])
        ring_kernel(dims, caps, refs[:N_INS], refs[N_INS], named)

    return pl.pallas_call(
        kernel,
        out_shape=jax.ShapeDtypeStruct((CHUNKS, n_grp, slots, wide), BF16),
        in_specs=[vmem] * 5 + [hbm] * 3,
        out_specs=vmem,
        scratch_shapes=leaves,
        compiler_params=pltpu.CompilerParams(
            collective_id=collective_id, has_side_effects=True, vmem_limit_bytes=60 * 1024 * 1024
        ),
        name=f"ring_exchange_{collective_id}",
    )(*operands)


def to_slots(values, half):
    n_grp = values.shape[0]
    ahead = jnp.flip(values[:, 1 : half + 1], 1).reshape(n_grp, CHUNKS, half // CHUNKS)
    behind = jnp.concatenate([values[:, :1], values[:, half + 1 :]], axis=1).reshape(n_grp, CHUNKS, half // CHUNKS)
    return jnp.transpose(jnp.concatenate([ahead, behind], axis=2), (1, 0, 2))


def from_slots(slots, half):
    n_grp = slots.shape[1]
    spc = half // CHUNKS
    slots = jnp.transpose(slots, (1, 0, 2))
    ahead = jnp.flip(slots[:, :, :spc].reshape(n_grp, half), 1)
    behind = slots[:, :, spc:].reshape(n_grp, half)
    return jnp.concatenate([behind[:, :1], ahead, behind[:, 1:]], axis=1)


def roll_columns(values, start):
    doubled = jnp.concatenate([values, values], axis=1)
    return lax.dynamic_slice_in_dim(doubled, start, values.shape[1], axis=1)


def prepare_kernel(dims, tok_rows, caps, lists_ref, flag_ref, picked_ref, hot_ref, pos_ref, src_pos_ref, got, send_sem, recv_sem):
    n_grp, n_seq, n_rep = dims
    half = n_seq // 2
    spc = half // CHUNKS
    slots = 2 * spc
    lanes = n_grp * slots
    n_experts = lists_ref.shape[0]
    rep, grp, col = lax.axis_index("rep"), lax.axis_index("grp"), lax.axis_index("seq")
    me = grp * n_seq + col

    def peer(step):
        return lax.rem(rep + step, n_rep)

    barrier = pltpu.get_barrier_semaphore()
    for step in range(1, n_rep):
        pl.semaphore_signal(barrier, inc=1, device_id={"rep": peer(step)}, device_id_type=MESH)

    def iota(shape, axis):
        return lax.broadcasted_iota(jnp.int32, shape, axis)

    def shift(n):
        return n.bit_length() - 1

    lists = jnp.transpose(lists_ref[...])
    owner = lists >> shift(tok_rows)
    src = owner >> shift(n_seq)
    column = owner & (n_seq - 1)
    expert = iota((1, n_experts), 1)
    dest = expert & (n_seq - 1)
    low = src < n_grp // 2
    gap_up = (dest - column) & (n_seq - 1)
    gap_down = (column - dest) & (n_seq - 1)
    d_up = jnp.where((gap_up < half) | ((gap_up == half) & low), gap_up, 0)
    d_down = jnp.where((gap_down < half) | ((gap_down == half) & ~low), gap_down, 0)

    def count(mask):
        return jnp.sum(mask.astype(jnp.int32), axis=0, keepdims=True)

    over = jnp.zeros((1, n_experts), jnp.int32)
    for k, cap in enumerate(caps):
        if cap < n_grp * (k + 1) - n_grp // 2:
            for distance in (d_up, d_down):
                over = jnp.maximum(over, count(distance >= half - k) - cap)
    bad = jnp.max(over.astype(F32), axis=1, keepdims=True)
    got[0] = jnp.broadcast_to(jnp.where(bad > 0.5, 0.0, 1.0), got.shape[1:])
    pl.semaphore_wait(barrier, n_rep - 1)

    def tell(step):
        return pltpu.make_async_remote_copy(
            src_ref=got.at[0],
            dst_ref=got.at[step],
            send_sem=send_sem.at[step],
            recv_sem=recv_sem.at[step],
            device_id={"rep": peer(step)},
            device_id_type=MESH,
        )

    for step in range(1, n_rep):
        tell(step).start()

    local = lists - me * tok_rows
    mine = (local >= 0) & (local < tok_rows)
    picked = jnp.max(jnp.where(mine, local, -1), axis=0, keepdims=True)
    picked_ref[...] = jnp.broadcast_to(picked, picked_ref.shape)

    shape = (n_experts, n_experts)
    row = iota(shape, 0)
    turn = row & (spc - 1)
    chunk = row >> shift(lanes)
    distance = half - spc * chunk - turn
    backward = (row >> shift(spc)) & 1
    rel = jnp.where(backward == 0, distance, jnp.where(distance == half, 0, n_seq - distance))
    wanted = ((row >> shift(slots)) & (n_grp - 1)) * n_seq + ((rel + col) & (n_seq - 1))
    perm = jnp.where(iota(shape, 1) == wanted, 1.0, 0.0).astype(BF16)
    hot_t = jnp.where(iota((tok_rows, n_experts), 0) == picked, 1.0, 0.0).astype(BF16)
    nt = (((1,), (1,)), ((), ()))
    hot_ref[...] = lax.dot_general(perm, hot_t, nt, preferred_element_type=F32).astype(BF16)

    here = column == col
    up_gap = (dest - col) & (n_seq - 1)
    down_gap = (col - dest) & (n_seq - 1)
    ahead_up = count(d_up > up_gap)
    ahead_down = count(d_down > down_gap)
    source = iota((n_grp, n_experts), 0)
    rows_up = jnp.zeros((n_grp, n_experts), jnp.int32)
    rows_down, rows_same = rows_up, rows_up
    for g in range(n_grp):
        present = count(here & (src == g))
        goes_up = (up_gap < half) | (up_gap == half) if g < n_grp // 2 else up_gap < half
        goes_down = down_gap < half if g < n_grp // 2 else (down_gap < half) | (down_gap == half)
        at_up = jnp.where(goes_up, present, 0)
        at_down = jnp.where(goes_down, present, 0)
        ahead_up = ahead_up + at_up
        ahead_down = ahead_down + at_down
        rows_up = jnp.where(source == g, at_up * ahead_up, rows_up)
        rows_down = jnp.where(source == g, at_down * ahead_down, rows_down)
        rows_same = jnp.where(source == g, present * (g + 1), rows_same)

    n_rows = src_pos_ref.shape[0]
    shape = (n_rows, n_experts)
    row = iota(shape, 0)
    hop = half - (row >> 1)
    lane = iota(shape, 1)
    base = grp * n_seq

    def pick(offset, on):
        wanted = base + ((col + offset) & (n_seq - 1))
        return jnp.where((lane == wanted) & on, 1.0, 0.0).astype(BF16)

    def take(select, values):
        return lax.dot_general(select, values.astype(F32).astype(BF16), nt, preferred_element_type=F32)

    stepping = row < n_seq
    places = take(pick(hop, stepping & ((row & 1) == 0)), rows_up)
    places = places + take(pick(n_seq - hop, stepping & ((row & 1) == 1)), rows_down)
    places = places + take(pick(0, row == n_seq), rows_same)
    src_pos_ref[...] = places.astype(jnp.int32) - 1
    shape = (n_grp, lanes)
    spread = jnp.where(iota(shape, 1) >> shift(slots) == iota(shape, 0), 1.0, 0.0).astype(BF16)
    wide = jnp.dot(places.astype(BF16), spread, preferred_element_type=F32).astype(jnp.int32)
    shape = (n_rows, lanes)
    row = iota(shape, 0)
    slot = ((row >> 1) & (spc - 1)) + spc * (row & 1)
    slot = jnp.where(row == 1, 0, jnp.where(row == n_seq, spc, slot))
    pos_ref[...] = jnp.where((iota(shape, 1) & (slots - 1)) == slot, wide, 0) - 1

    for step in range(1, n_rep):
        tell(step).wait()
    flag = got[0]
    for step in range(1, n_rep):
        flag = flag * got[step]
    flag_ref[...] = flag


def prepare(dims, tok_rows, caps, lists):
    n_grp, n_seq, n_rep = dims
    n_experts = lists.shape[0]
    n_rows = n_seq + 8
    lanes = n_grp * 2 * (n_seq // 2 // CHUNKS)
    vmem = pl.BlockSpec(memory_space=pltpu.VMEM)
    return pl.pallas_call(
        functools.partial(prepare_kernel, dims, tok_rows, caps),
        out_shape=(
            jax.ShapeDtypeStruct((8, 128), F32),
            jax.ShapeDtypeStruct((8, n_experts), jnp.int32),
            jax.ShapeDtypeStruct((n_experts, tok_rows), BF16),
            jax.ShapeDtypeStruct((n_rows, lanes), jnp.int32),
            jax.ShapeDtypeStruct((n_rows, n_grp), jnp.int32),
        ),
        in_specs=[vmem],
        out_specs=(vmem,) * 5,
        scratch_shapes=[
            pltpu.VMEM((n_rep, 8, 128), F32),
            pltpu.SemaphoreType.DMA((n_rep,)),
            pltpu.SemaphoreType.DMA((n_rep,)),
        ],
        compiler_params=pltpu.CompilerParams(
            collective_id=2, has_side_effects=True, vmem_limit_bytes=16 * 1024 * 1024
        ),
        name="prepare",
    )(lists)


def body(tokens, token_cot, router_logits, token_lists, w_gate, w_up, w_down):
    n_grp = lax.axis_size("grp")
    n_seq = lax.axis_size("seq")
    half = n_seq // 2
    col = lax.axis_index("seq")
    tok_rows, width = tokens.shape
    n_experts, cap = token_lists.shape
    dims = (n_grp, n_seq, width, 128)

    token_ids = jnp.arange(tok_rows, dtype=jnp.int32)
    full = tuple(to_grain(n_grp * k - n_grp // 2) for k in range(1, half + 1))
    usual = usual_caps(n_grp, n_seq)
    flag, picked, hot, pos, src_pos = prepare((n_grp, n_seq, lax.axis_size("rep")), tok_rows, usual, token_lists)
    picked = picked[0]
    fin = lax.cond(
        flag[0, 0] > 0.5,
        functools.partial(exchange, dims, usual, 0),
        functools.partial(exchange, dims, full, 1),
        tokens, token_cot, hot, pos, src_pos, w_gate[0], w_up[0], w_down[0],
    )
    fin = fin.reshape(n_experts, width + dims[3])

    gate_vals = jax.nn.sigmoid(router_logits)
    select = picked[None, :] == token_ids[:, None]
    own_gates = jnp.sum(jnp.where(select, gate_vals, 0.0), axis=0)
    gate_slots = to_slots(roll_columns(own_gates.reshape(n_grp, n_seq), col), half).reshape(n_experts)
    weight = hot.astype(F32) * gate_slots[:, None]
    token_grad = lax.dot_general(
        weight,
        fin[:, :width].astype(F32),
        (((0,), (0,)), ((), ())),
        precision=lax.Precision.HIGHEST,
        preferred_element_type=F32,
    )
    back_gates = from_slots(fin[:, width].reshape(CHUNKS, n_grp, 2 * (half // CHUNKS)), half)
    back_gates = roll_columns(back_gates, lax.rem(n_seq - col, n_seq)).reshape(n_experts).astype(F32)
    logit_grad = jnp.where(select, gate_vals * (1.0 - gate_vals) * back_gates[None, :], 0.0)
    return (token_grad.astype(BF16), logit_grad)


def solution(mesh):
    in_specs = (
        P(("rep", "grp", "seq"), None),
        P(("rep", "grp", "seq"), None),
        P(("rep", "grp", "seq"), None),
        P("rep", None),
        P(("grp", "seq"), None, None),
        P(("grp", "seq"), None, None),
        P(("grp", "seq"), None, None),
    )
    out_specs = (P(("rep", "grp", "seq"), None), P(("rep", "grp", "seq"), None))
    return jax.shard_map(body, mesh=mesh, in_specs=in_specs, out_specs=out_specs, check_vma=False)
```

```python
import functools
import math

import jax
import jax.numpy as jnp
from jax import lax
from jax.experimental import pallas as pl
from jax.experimental.pallas import tpu as pltpu
from jax.sharding import PartitionSpec as P

MESH = pl.DeviceIdType.MESH
BF16 = jnp.bfloat16
F32 = jnp.float32
CHUNKS = 4
GRAIN = 4
HALVES = 2
PARTS = 4


def to_grain(n):
    return -(-n // GRAIN) * GRAIN


def usual_caps(n_grp, n_seq):
    total = n_grp * n_seq
    caps = []
    for k in range(1, n_seq // 2 + 1):
        slots = n_grp * k - n_grp // 2
        spread = math.sqrt(slots * (total - slots) / (4 * total))
        caps.append(-(-math.floor(min(slots, slots / 2 + 4.75 * spread)) // GRAIN) * GRAIN)
    return tuple(max(cap, caps[0]) for cap in caps)


def one_hot_rows(pos_row, rows):
    row_ids = lax.broadcasted_iota(jnp.int32, (rows, pos_row.shape[1]), 0)
    return jnp.where(row_ids == pos_row, 1.0, 0.0).astype(BF16)


def part_columns(width, tail):
    size = width // PARTS
    return [(part * size, size + (tail if part == PARTS - 1 else 0)) for part in range(PARTS)]


def ring_kernel(dims, caps, ins, fin_ref, scratch):
    n_grp, n_seq, width, tail = dims
    half = n_seq // 2
    spc = half // CHUNKS
    slots = 2 * spc
    wide = width + tail
    lanes = n_grp * slots
    x_ref, g_ref, hot_ref, pos_ref, src_pos_ref, wg_hbm, wu_hbm, wd_hbm = ins
    packs, backs, dx = scratch["packs"], scratch["backs"], scratch["dx"]
    wg_ref, wu_ref, wd_ref = scratch["wg"], scratch["wu"], scratch["wd"]
    send_buf, own, fresh, final, flat = (scratch[name] for name in ("send_buf", "own", "fresh", "final", "flat"))
    gate_scr, up_scr = scratch["gate"], scratch["up"]
    dropped, back_send = scratch["dropped"], scratch["back_send"]
    parts = part_columns(width, tail)
    grp = lax.axis_index("grp")
    col = lax.axis_index("seq")
    cap_last = caps[half - 1]
    col_tile = min(width // PARTS, 512)
    n_tiles = width // col_tile

    def tile_cols(i):
        return pl.ds(pl.multiple_of(i * col_tile, col_tile), col_tile)

    def neighbour(direction):
        return lax.rem(col + 1 + direction * (n_seq - 2), n_seq)

    def peer(step):
        return lax.rem(grp + step, n_grp)

    weights = [
        pltpu.make_async_copy(wg_hbm, wg_ref, scratch["w_sem"].at[0]),
        pltpu.make_async_copy(wu_hbm, wu_ref, scratch["w_sem"].at[1]),
        pltpu.make_async_copy(wd_hbm, wd_ref, scratch["w_sem"].at[2]),
    ]

    barrier = pltpu.get_barrier_semaphore()
    for step in range(1, n_grp):
        pl.semaphore_signal(barrier, inc=1, device_id={"grp": peer(step)}, device_id_type=MESH)
    for direction in range(2):
        pl.semaphore_signal(barrier, inc=1, device_id={"seq": neighbour(direction)}, device_id_type=MESH)

    def pick(source, arr, chunk):
        hot = hot_ref[pl.ds(chunk * lanes, lanes), :]

        def tile(i, carry):
            cols = tile_cols(i)
            rows = jnp.dot(hot, source[:, cols], preferred_element_type=F32).astype(BF16)
            send_buf[arr, chunk, :, :, cols] = rows.reshape(n_grp, slots, col_tile)
            return carry

        lax.fori_loop(0, n_tiles, tile, 0)

    def stage_copy(arr, chunk, step, src_grp):
        return pltpu.make_async_remote_copy(
            src_ref=send_buf.at[arr, chunk, peer(step)],
            dst_ref=own.at[arr, chunk, src_grp],
            send_sem=scratch["s1_send"].at[arr, chunk, step],
            recv_sem=scratch["s1_recv"].at[arr, chunk, step],
            device_id={"grp": peer(step)},
            device_id_type=MESH,
        )

    def stage_local(arr, chunk):
        return pltpu.make_async_copy(
            send_buf.at[arr, chunk, grp], own.at[arr, chunk, grp], scratch["loc_sem"].at[arr, chunk]
        )

    def stage_wait(arr, chunk):
        stage_local(arr, chunk).wait()
        for step in range(1, n_grp):
            stage_copy(arr, chunk, step, lax.rem(grp + n_grp - step, n_grp)).wait_recv()

    pick(x_ref, 0, 0)
    pl.semaphore_wait(barrier, n_grp + 1)
    for chunk, arr in [(chunk, arr) for chunk in range(CHUNKS) for arr in range(2)]:
        if chunk or arr:
            pick((x_ref, g_ref)[arr], arr, chunk)
        stage_local(arr, chunk).start()
        for step in range(1, n_grp):
            stage_copy(arr, chunk, step, grp).start()
    for copy in weights:
        copy.start()

    half_tiles = n_tiles // HALVES

    def send_packet(step, stream, direction):
        if step + 1 < half:
            dst = packs[step + 1].at[stream, direction, pl.ds(0, caps[step] // GRAIN)]
        else:
            dst = final.at[stream, pl.ds(direction * cap_last // GRAIN, cap_last // GRAIN)]
        return pltpu.make_async_remote_copy(
            src_ref=packs[step].at[stream, direction],
            dst_ref=dst,
            send_sem=scratch["d_send"].at[stream, direction, step],
            recv_sem=scratch["d_recv"].at[stream, direction, step],
            device_id={"seq": neighbour(direction)},
            device_id_type=MESH,
        )

    def make_fresh(step, stream):
        arr, piece = divmod(stream, HALVES)
        cap = caps[step]
        prev_cap = caps[step - 1] if step else 0

        def one(direction, carry):
            hot = one_hot_rows(pos_ref[pl.ds(2 * step + direction, 1), :], cap)

            def tile(i, inner):
                cols = tile_cols(i)
                from_cols = tile_cols(i + piece * half_tiles)
                mine = own[arr, step // spc, :, :, from_cols].reshape(lanes, col_tile)
                rows = jnp.dot(hot, mine, preferred_element_type=F32).astype(BF16)
                rows = rows.reshape(cap // GRAIN, GRAIN, col_tile)
                held = prev_cap // GRAIN
                if held:
                    fresh[stream, direction, pl.ds(0, held), :, cols] = rows[:held]
                if cap > prev_cap:
                    packs[step][stream, direction, pl.ds(held, cap // GRAIN - held), :, cols] = rows[held:]
                return inner

            lax.fori_loop(0, half_tiles, tile, 0)
            return carry

        lax.fori_loop(0, 2, one, 0)

    for step in range(half):
        for stream in range(2 * HALVES):
            arr, piece = divmod(stream, HALVES)
            if step == 0:
                if piece == 0:
                    stage_wait(arr, 0)
                make_fresh(0, stream)

            def hop(direction, carry, step=step, stream=stream):
                if step:
                    prev = pl.ds(0, caps[step - 1] // GRAIN)
                    send_packet(step - 1, stream, direction).wait_recv()
                    packs[step][stream, direction, prev] += fresh[stream, direction, prev]
                send_packet(step, stream, direction).start()
                return carry

            lax.fori_loop(0, 2, hop, 0)
            if step + 1 < half:
                if (step + 1) % spc == 0 and piece == 0:
                    stage_wait(arr, (step + 1) // spc)
                make_fresh(step + 1, stream)

    same_hot = one_hot_rows(pos_ref[pl.ds(2 * half, 1), :], 16)
    for arr in range(2):

        def same_tile(i, inner, arr=arr):
            cols = tile_cols(i)
            mine = own[arr, 0, :, :, cols].reshape(lanes, col_tile)
            rows = jnp.dot(same_hot, mine, preferred_element_type=F32)
            flat[arr, pl.ds(2 * cap_last, 16), cols] = rows.astype(BF16)
            return inner

        lax.fori_loop(0, n_tiles, same_tile, 0)

    for copy in weights:
        copy.wait()
    def take_packets(arr):
        for piece in range(HALVES):
            stream = arr * HALVES + piece
            for direction in range(2):
                send_packet(half - 1, stream, direction).wait_recv()

            def tile(i, carry, stream=stream, piece=piece):
                rows = final[stream, :, :, tile_cols(i)].reshape(2 * cap_last, col_tile)
                flat[arr, pl.ds(0, 2 * cap_last), tile_cols(i + piece * half_tiles)] = rows
                return carry

            lax.fori_loop(0, half_tiles, tile, 0)

    take_packets(0)
    gate_scr[...] = jnp.dot(flat[0], wg_ref[...], preferred_element_type=F32)
    up_scr[...] = jnp.dot(flat[0], wu_ref[...], preferred_element_type=F32)
    take_packets(1)
    nt = (((1,), (1,)), ((), ()))
    d_hidden = lax.dot_general(flat[1], wd_ref[...], nt, preferred_element_type=F32)
    gate_pre = gate_scr[...]
    up_pre = up_scr[...]
    sig = jax.nn.sigmoid(gate_pre)
    activated = gate_pre * sig
    hidden = (activated * up_pre).astype(BF16).astype(F32)
    gate_grad = jnp.sum(hidden * d_hidden, axis=1, keepdims=True)
    scratch["d_gate"][...] = (d_hidden * up_pre * sig * (1.0 + gate_pre * (1.0 - sig))).astype(BF16)
    scratch["d_up"][...] = (d_hidden * activated).astype(BF16)
    n_rows = gate_grad.shape[0]
    gates = jnp.broadcast_to(gate_grad, (n_rows, tail)).astype(BF16)
    dx[PARTS - 1][:, :, width // PARTS :] = gates.reshape(n_rows // GRAIN, GRAIN, tail)

    def send_back(step, part, direction):
        cap = caps[half - 1 - step]
        if step == 0:
            src = dx[part].at[pl.ds(direction * cap_last // GRAIN, cap_last // GRAIN)]
        else:
            src = backs[part][step - 1].at[direction, pl.ds(0, cap // GRAIN)]
        return pltpu.make_async_remote_copy(
            src_ref=src,
            dst_ref=backs[part][step].at[direction],
            send_sem=scratch["r_send"].at[part, direction, step],
            recv_sem=scratch["r_recv"].at[part, direction, step],
            device_id={"seq": neighbour(1 - direction)},
            device_id_type=MESH,
        )

    for part in range(PARTS):

        def dx_tile(i, carry, part=part):
            w_rows = tile_cols(i + part * (n_tiles // PARTS))
            rows = lax.dot_general(scratch["d_gate"][...], wg_ref[w_rows, :], nt, preferred_element_type=F32)
            rows = rows + lax.dot_general(scratch["d_up"][...], wu_ref[w_rows, :], nt, preferred_element_type=F32)
            dx[part][:, :, tile_cols(i)] = rows.astype(BF16).reshape(n_rows // GRAIN, GRAIN, col_tile)
            return carry

        lax.fori_loop(0, n_tiles // PARTS, dx_tile, 0)
        for direction in range(2):
            send_back(0, part, direction).start()

    def home_copy(chunk, step, src_grp):
        return pltpu.make_async_remote_copy(
            src_ref=back_send.at[chunk, peer(step)],
            dst_ref=fin_ref.at[chunk, src_grp],
            send_sem=scratch["s2_send"].at[chunk, step],
            recv_sem=scratch["s2_recv"].at[chunk, step],
            device_id={"grp": peer(step)},
            device_id_type=MESH,
        )

    def home_local(chunk):
        return pltpu.make_async_copy(back_send.at[chunk, grp], fin_ref.at[chunk, grp], scratch["loc_sem"].at[2, chunk])

    tn = (((0,), (0,)), ((), ()))

    def drop(row, cap, rows, slot, part, add=False):
        hot = one_hot_rows(src_pos_ref[pl.ds(row, 1), :n_grp], cap)
        first, size = parts[part]
        kept = lax.dot_general(hot, rows.reshape(cap, size), tn, preferred_element_type=F32)
        at = pl.ds(slot * n_grp, n_grp)
        if add:
            kept = kept + dropped[at, pl.ds(first, size)]
        dropped[at, pl.ds(first, size)] = kept

    def regroup(chunk):
        shape = (lanes, lanes)
        to = lax.broadcasted_iota(jnp.int32, shape, 0)
        frm = lax.broadcasted_iota(jnp.int32, shape, 1)
        perm = jnp.where((to // slots == frm % n_grp) & (to % slots == frm // n_grp), 1.0, 0.0).astype(BF16)

        def put(cols, size):
            rows = jnp.dot(perm, dropped[:, cols].astype(BF16), preferred_element_type=F32).astype(BF16)
            back_send[chunk, :, :, cols] = rows.reshape(n_grp, slots, size)

        def tile(i, carry):
            put(tile_cols(i), col_tile)
            return carry

        lax.fori_loop(0, n_tiles, tile, 0)
        put(pl.ds(width, tail), tail)

    for step in range(half):
        k = half - 1 - step
        chunk = k // spc
        for part in range(PARTS):
            for direction in range(2):
                send_back(step, part, direction).wait_recv()
                if step + 1 < half:
                    send_back(step + 1, part, direction).start()
            if k == spc - 1:
                drop(2 * half, 16, dx[part][pl.ds(2 * cap_last // GRAIN, 16 // GRAIN)], spc, part)
            for direction in range(2):
                slot = k % spc + (spc if direction and k else 0)
                drop(2 * k + direction, caps[k], backs[part][step][direction], slot, part, bool(direction and k == 0))
        if k % spc == 0:
            regroup(chunk)
            home_local(chunk).start()
            for s in range(1, n_grp):
                home_copy(chunk, s, grp).start()

    for arr in range(2):
        for chunk in range(CHUNKS):
            for s in range(1, n_grp):
                stage_copy(arr, chunk, s, grp).wait_send()
    for step in range(half):
        for direction in range(2):
            for stream in range(2 * HALVES):
                send_packet(step, stream, direction).wait_send()
            for part in range(PARTS):
                send_back(step, part, direction).wait_send()
    for chunk in reversed(range(CHUNKS)):
        home_local(chunk).wait()
        for s in range(1, n_grp):
            home_copy(chunk, s, grp).wait_send()
            home_copy(chunk, s, lax.rem(grp + n_grp - s, n_grp)).wait_recv()


N_INS = 8


def exchange(dims, caps, collective_id, *operands):
    n_grp, n_seq, width, tail = dims
    half = n_seq // 2
    w_gate, w_up, w_down = operands[5:]
    ff = w_gate.shape[1]
    wide = width + tail
    rows = 2 * caps[-1] + 16
    slots = 2 * (half // CHUNKS)
    lanes = n_grp * slots
    streams, piece, parts = 2 * HALVES, width // HALVES, part_columns(width, tail)
    dma = pltpu.SemaphoreType.DMA
    vmem = pl.BlockSpec(memory_space=pltpu.VMEM)
    hbm = pl.BlockSpec(memory_space=pl.ANY)
    scratch = {
        "wg": pltpu.VMEM(w_gate.shape, BF16),
        "wu": pltpu.VMEM(w_up.shape, BF16),
        "wd": pltpu.VMEM(w_down.shape, BF16),
        "send_buf": pltpu.VMEM((2, CHUNKS, n_grp, slots, width), BF16),
        "own": pltpu.VMEM((2, CHUNKS, n_grp, slots, width), BF16),
        "packs": [pltpu.VMEM((streams, 2, cap // GRAIN, GRAIN, piece), BF16) for cap in caps],
        "fresh": pltpu.VMEM((streams, 2, caps[-2] // GRAIN, GRAIN, piece), BF16),
        "final": pltpu.VMEM((streams, 2 * caps[-1] // GRAIN, GRAIN, piece), BF16),
        "flat": pltpu.VMEM((2, rows, width), BF16),
        "gate": pltpu.VMEM((rows, ff), F32),
        "up": pltpu.VMEM((rows, ff), F32),
        "d_gate": pltpu.VMEM((rows, ff), BF16),
        "d_up": pltpu.VMEM((rows, ff), BF16),
        "dx": [pltpu.VMEM((rows // GRAIN, GRAIN, size), BF16) for _, size in parts],
        "backs": [
            [pltpu.VMEM((2, cap // GRAIN, GRAIN, size), BF16) for cap in reversed(caps)] for _, size in parts
        ],
        "dropped": pltpu.VMEM((lanes, wide), F32),
        "back_send": pltpu.VMEM((CHUNKS, n_grp, slots, wide), BF16),
        "w_sem": dma((3,)),
        "s1_send": dma((2, CHUNKS, n_grp)),
        "s1_recv": dma((2, CHUNKS, n_grp)),
        "d_send": dma((streams, 2, half)),
        "d_recv": dma((streams, 2, half)),
        "r_send": dma((PARTS, 2, half)),
        "r_recv": dma((PARTS, 2, half)),
        "s2_send": dma((CHUNKS, n_grp)),
        "s2_recv": dma((CHUNKS, n_grp)),
        "loc_sem": dma((3, CHUNKS)),
    }
    leaves, tree = jax.tree.flatten(scratch, is_leaf=lambda leaf: not isinstance(leaf, (dict, list)))

    def kernel(*refs):
        named = jax.tree.unflatten(tree, refs[N_INS + 1 :])
        ring_kernel(dims, caps, refs[:N_INS], refs[N_INS], named)

    return pl.pallas_call(
        kernel,
        out_shape=jax.ShapeDtypeStruct((CHUNKS, n_grp, slots, wide), BF16),
        in_specs=[vmem] * 5 + [hbm] * 3,
        out_specs=vmem,
        scratch_shapes=leaves,
        compiler_params=pltpu.CompilerParams(
            collective_id=collective_id, has_side_effects=True, vmem_limit_bytes=60 * 1024 * 1024
        ),
        name=f"ring_exchange_{collective_id}",
    )(*operands)


def to_slots(values, half):
    n_grp = values.shape[0]
    ahead = jnp.flip(values[:, 1 : half + 1], 1).reshape(n_grp, CHUNKS, half // CHUNKS)
    behind = jnp.concatenate([values[:, :1], values[:, half + 1 :]], axis=1).reshape(n_grp, CHUNKS, half // CHUNKS)
    return jnp.transpose(jnp.concatenate([ahead, behind], axis=2), (1, 0, 2))


def from_slots(slots, half):
    n_grp = slots.shape[1]
    spc = half // CHUNKS
    slots = jnp.transpose(slots, (1, 0, 2))
    ahead = jnp.flip(slots[:, :, :spc].reshape(n_grp, half), 1)
    behind = slots[:, :, spc:].reshape(n_grp, half)
    return jnp.concatenate([behind[:, :1], ahead, behind[:, 1:]], axis=1)


def roll_columns(values, start):
    doubled = jnp.concatenate([values, values], axis=1)
    return lax.dynamic_slice_in_dim(doubled, start, values.shape[1], axis=1)


def prepare_kernel(dims, tok_rows, caps, lists_ref, flag_ref, picked_ref, hot_ref, pos_ref, src_pos_ref, got, send_sem, recv_sem):
    n_grp, n_seq, n_rep = dims
    half = n_seq // 2
    spc = half // CHUNKS
    slots = 2 * spc
    lanes = n_grp * slots
    n_experts = lists_ref.shape[0]
    rep, grp, col = lax.axis_index("rep"), lax.axis_index("grp"), lax.axis_index("seq")
    me = grp * n_seq + col

    def peer(step):
        return lax.rem(rep + step, n_rep)

    barrier = pltpu.get_barrier_semaphore()
    for step in range(1, n_rep):
        pl.semaphore_signal(barrier, inc=1, device_id={"rep": peer(step)}, device_id_type=MESH)

    def iota(shape, axis):
        return lax.broadcasted_iota(jnp.int32, shape, axis)

    def shift(n):
        return n.bit_length() - 1

    lists = jnp.transpose(lists_ref[...])
    owner = lists >> shift(tok_rows)
    src = owner >> shift(n_seq)
    column = owner & (n_seq - 1)
    expert = iota((1, n_experts), 1)
    dest = expert & (n_seq - 1)
    low = src < n_grp // 2
    gap_up = (dest - column) & (n_seq - 1)
    gap_down = (column - dest) & (n_seq - 1)
    d_up = jnp.where((gap_up < half) | ((gap_up == half) & low), gap_up, 0)
    d_down = jnp.where((gap_down < half) | ((gap_down == half) & ~low), gap_down, 0)

    def count(mask):
        return jnp.sum(mask.astype(jnp.int32), axis=0, keepdims=True)

    over = jnp.zeros((1, n_experts), jnp.int32)
    for k, cap in enumerate(caps):
        if cap < n_grp * (k + 1) - n_grp // 2:
            for distance in (d_up, d_down):
                over = jnp.maximum(over, count(distance >= half - k) - cap)
    bad = jnp.max(over.astype(F32), axis=1, keepdims=True)
    got[0] = jnp.broadcast_to(jnp.where(bad > 0.5, 0.0, 1.0), got.shape[1:])
    pl.semaphore_wait(barrier, n_rep - 1)

    def tell(step):
        return pltpu.make_async_remote_copy(
            src_ref=got.at[0],
            dst_ref=got.at[step],
            send_sem=send_sem.at[step],
            recv_sem=recv_sem.at[step],
            device_id={"rep": peer(step)},
            device_id_type=MESH,
        )

    for step in range(1, n_rep):
        tell(step).start()

    local = lists - me * tok_rows
    mine = (local >= 0) & (local < tok_rows)
    picked = jnp.max(jnp.where(mine, local, -1), axis=0, keepdims=True)
    picked_ref[...] = jnp.broadcast_to(picked, picked_ref.shape)

    shape = (n_experts, n_experts)
    row = iota(shape, 0)
    turn = row & (spc - 1)
    chunk = row >> shift(lanes)
    distance = half - spc * chunk - turn
    backward = (row >> shift(spc)) & 1
    rel = jnp.where(backward == 0, distance, jnp.where(distance == half, 0, n_seq - distance))
    wanted = ((row >> shift(slots)) & (n_grp - 1)) * n_seq + ((rel + col) & (n_seq - 1))
    perm = jnp.where(iota(shape, 1) == wanted, 1.0, 0.0).astype(BF16)
    hot_t = jnp.where(iota((tok_rows, n_experts), 0) == picked, 1.0, 0.0).astype(BF16)
    nt = (((1,), (1,)), ((), ()))
    hot_ref[...] = lax.dot_general(perm, hot_t, nt, preferred_element_type=F32).astype(BF16)

    here = column == col
    up_gap = (dest - col) & (n_seq - 1)
    down_gap = (col - dest) & (n_seq - 1)
    ahead_up = count(d_up > up_gap)
    ahead_down = count(d_down > down_gap)
    source = iota((n_grp, n_experts), 0)
    rows_up = jnp.zeros((n_grp, n_experts), jnp.int32)
    rows_down, rows_same = rows_up, rows_up
    for g in range(n_grp):
        present = count(here & (src == g))
        goes_up = (up_gap < half) | (up_gap == half) if g < n_grp // 2 else up_gap < half
        goes_down = down_gap < half if g < n_grp // 2 else (down_gap < half) | (down_gap == half)
        at_up = jnp.where(goes_up, present, 0)
        at_down = jnp.where(goes_down, present, 0)
        ahead_up = ahead_up + at_up
        ahead_down = ahead_down + at_down
        rows_up = jnp.where(source == g, at_up * ahead_up, rows_up)
        rows_down = jnp.where(source == g, at_down * ahead_down, rows_down)
        rows_same = jnp.where(source == g, present * (g + 1), rows_same)

    n_rows = src_pos_ref.shape[0]
    shape = (n_rows, n_experts)
    row = iota(shape, 0)
    hop = half - (row >> 1)
    lane = iota(shape, 1)
    base = grp * n_seq

    def pick(offset, on):
        wanted = base + ((col + offset) & (n_seq - 1))
        return jnp.where((lane == wanted) & on, 1.0, 0.0).astype(BF16)

    def take(select, values):
        return lax.dot_general(select, values.astype(F32).astype(BF16), nt, preferred_element_type=F32)

    stepping = row < n_seq
    places = take(pick(hop, stepping & ((row & 1) == 0)), rows_up)
    places = places + take(pick(n_seq - hop, stepping & ((row & 1) == 1)), rows_down)
    places = places + take(pick(0, row == n_seq), rows_same)
    src_pos_ref[...] = places.astype(jnp.int32) - 1
    shape = (n_grp, lanes)
    spread = jnp.where(iota(shape, 1) >> shift(slots) == iota(shape, 0), 1.0, 0.0).astype(BF16)
    wide = jnp.dot(places.astype(BF16), spread, preferred_element_type=F32).astype(jnp.int32)
    shape = (n_rows, lanes)
    row = iota(shape, 0)
    slot = ((row >> 1) & (spc - 1)) + spc * (row & 1)
    slot = jnp.where(row == 1, 0, jnp.where(row == n_seq, spc, slot))
    pos_ref[...] = jnp.where((iota(shape, 1) & (slots - 1)) == slot, wide, 0) - 1

    for step in range(1, n_rep):
        tell(step).wait()
    flag = got[0]
    for step in range(1, n_rep):
        flag = flag * got[step]
    flag_ref[...] = flag


def prepare(dims, tok_rows, caps, lists):
    n_grp, n_seq, n_rep = dims
    n_experts = lists.shape[0]
    n_rows = n_seq + 8
    lanes = n_grp * 2 * (n_seq // 2 // CHUNKS)
    vmem = pl.BlockSpec(memory_space=pltpu.VMEM)
    return pl.pallas_call(
        functools.partial(prepare_kernel, dims, tok_rows, caps),
        out_shape=(
            jax.ShapeDtypeStruct((8, 128), F32),
            jax.ShapeDtypeStruct((8, n_experts), jnp.int32),
            jax.ShapeDtypeStruct((n_experts, tok_rows), BF16),
            jax.ShapeDtypeStruct((n_rows, lanes), jnp.int32),
            jax.ShapeDtypeStruct((n_rows, n_grp), jnp.int32),
        ),
        in_specs=[vmem],
        out_specs=(vmem,) * 5,
        scratch_shapes=[
            pltpu.VMEM((n_rep, 8, 128), F32),
            pltpu.SemaphoreType.DMA((n_rep,)),
            pltpu.SemaphoreType.DMA((n_rep,)),
        ],
        compiler_params=pltpu.CompilerParams(
            collective_id=2, has_side_effects=True, vmem_limit_bytes=16 * 1024 * 1024
        ),
        name="prepare",
    )(lists)


def body(tokens, token_cot, router_logits, token_lists, w_gate, w_up, w_down):
    n_grp = lax.axis_size("grp")
    n_seq = lax.axis_size("seq")
    half = n_seq // 2
    col = lax.axis_index("seq")
    tok_rows, width = tokens.shape
    n_experts, cap = token_lists.shape
    dims = (n_grp, n_seq, width, 128)

    token_ids = jnp.arange(tok_rows, dtype=jnp.int32)
    full = tuple(to_grain(n_grp * k - n_grp // 2) for k in range(1, half + 1))
    usual = usual_caps(n_grp, n_seq)
    flag, picked, hot, pos, src_pos = prepare((n_grp, n_seq, lax.axis_size("rep")), tok_rows, usual, token_lists)
    picked = picked[0]
    fin = lax.cond(
        flag[0, 0] > 0.5,
        functools.partial(exchange, dims, usual, 0),
        functools.partial(exchange, dims, full, 1),
        tokens, token_cot, hot, pos, src_pos, w_gate[0], w_up[0], w_down[0],
    )
    fin = fin.reshape(n_experts, width + dims[3])

    gate_vals = jax.nn.sigmoid(router_logits)
    select = picked[None, :] == token_ids[:, None]
    own_gates = jnp.sum(jnp.where(select, gate_vals, 0.0), axis=0)
    gate_slots = to_slots(roll_columns(own_gates.reshape(n_grp, n_seq), col), half).reshape(n_experts)
    weight = hot.astype(F32) * gate_slots[:, None]
    token_grad = lax.dot_general(
        weight,
        fin[:, :width].astype(F32),
        (((0,), (0,)), ((), ())),
        precision=lax.Precision.HIGHEST,
        preferred_element_type=F32,
    )
    back_gates = from_slots(fin[:, width].reshape(CHUNKS, n_grp, 2 * (half // CHUNKS)), half)
    back_gates = roll_columns(back_gates, lax.rem(n_seq - col, n_seq)).reshape(n_experts).astype(F32)
    logit_grad = jnp.where(select, gate_vals * (1.0 - gate_vals) * back_gates[None, :], 0.0)
    return (token_grad.astype(BF16), logit_grad)


def solution(mesh):
    in_specs = (
        P(("rep", "grp", "seq"), None),
        P(("rep", "grp", "seq"), None),
        P(("rep", "grp", "seq"), None),
        P("rep", None),
        P(("grp", "seq"), None, None),
        P(("grp", "seq"), None, None),
        P(("grp", "seq"), None, None),
    )
    out_specs = (P(("rep", "grp", "seq"), None), P(("rep", "grp", "seq"), None))
    return jax.shard_map(body, mesh=mesh, in_specs=in_specs, out_specs=out_specs, check_vma=False)
```
